32 devices in a mesh: dp: 2 (over y), row: 4 (over z), col: 4 (over x, core).
Axes of the slice: x: 2, y: 2, z: 4, core: 2. Of those that a mesh axis runs over, the one named last changes fastest.
Arguments:
- inputs: bfloat16 [2, 256, 128, 512], P('dp', None, 'row', 'col'), may hold values from -6 to 6
- reduce_weight: bfloat16 [64, 256], replicated, may hold values from -0.375 to 0.375
- spatial_weight: bfloat16 [3, 3, 64, 64], replicated, may hold values from -0.25 to 0.25
- expand_weight: bfloat16 [256, 64], replicated, may hold values from -0.75 to 0.75
- class_weight: bfloat16 [3, 3, 135, 256], replicated, may hold values from -0.125 to 0.125
- anchor_labels: int32 [2, 9, 128, 512], P('dp', None, 'row', 'col'), may hold values from 0 to 15, as said below
- anchor_mask: int32 [2, 9, 128, 512], P('dp', None, 'row', 'col'), may hold values from 0 to 1, as said below
Outputs:
- loss: float32 [], replicated
- grad_reduce: float32 [64, 256], replicated
- grad_spatial: float32 [3, 3, 64, 64], replicated
- grad_expand: float32 [256, 64], replicated
- grad_class: float32 [3, 3, 135, 256], replicated
The draws below stay inside these ranges and needn't reach their ends.
Inputs may be any that keep to these rules, and one draw needn't show every extreme that they name: `anchor_labels`: labels are 0 to 15; anchor 0 at the first row and column of every tile is positive. `anchor_mask`: every anchor with a label above 0 has mask 1.
All inputs are finite; a program needn't handle non-finite values.
Results may differ from the reference program's by a relative error of at most 0.0034.
Values may be sent and summed in bfloat16 or wider, within the bound.
A program may use at most 128 MiB of HBM per device.

```python
import jax
import jax.numpy as jnp
from jax import lax

C = 256
MID = 64
A = 9
K = 15
TILES = 2
H = 128
W = 512


def anchor_pair(key):
    label_key = jax.random.fold_in(key, 11)
    class_key = jax.random.fold_in(key, 12)
    valid_key = jax.random.fold_in(key, 13)
    shape = (TILES, A, H, W)
    tile_index = jnp.arange(TILES, dtype=jnp.int32)[:, None, None, None]
    row_index = jnp.arange(H, dtype=jnp.int32)[None, None, :, None]
    place = tile_index * H + row_index
    threshold = 10 + 20 * place // max(TILES * H - 1, 1)
    rolled = jax.random.randint(label_key, shape, 0, 1000, dtype=jnp.int32)
    classes = jax.random.randint(class_key, shape, 1, K + 1, dtype=jnp.int32)
    labels = jnp.where(rolled < threshold, classes, 0)
    anchor_index = jnp.arange(A, dtype=jnp.int32)[None, :, None, None]
    column_index = jnp.arange(W, dtype=jnp.int32)[None, None, None, :]
    forced = (anchor_index == 0) & (row_index == 0) & (column_index == 0)
    labels = jnp.where(forced, jnp.maximum(classes, 1), labels)
    valid = jax.random.randint(valid_key, shape, 0, 100, dtype=jnp.int32) < 85
    mask = jnp.where((labels > 0) | valid, 1, 0).astype(jnp.int32)
    return (labels.astype(jnp.int32), mask)


def draw_anchor_labels(key, part):
    return anchor_pair(key)[0]


def draw_anchor_mask(key, part):
    return anchor_pair(key)[1]


def levels(key, extent, split, smallest, top_value):
    level = 1.0
    for axis_at, blocks in split:
        steps = jax.random.uniform(jax.random.fold_in(jax.random.fold_in(key, 6), axis_at), (blocks,), jnp.float32, smallest / len(split), top_value / len(split))
        level = level * jnp.repeat(jnp.exp(steps), extent[axis_at] // blocks).reshape((-1,) + (1,) * (len(extent) - 1 - axis_at))
    return level


def scatter_about(key, shape, width, bound, shards=(), kind=jnp.bfloat16):
    entries = width * jax.random.normal(key, shape, jnp.float32)
    if shards:
        entries = entries * levels(key, shape, shards, -0.22, 0.18)
    return jnp.clip(entries, -bound, bound).astype(kind)


def setup_inputs(seed: int = 0) -> dict:
    arg_keys = jax.random.split(jax.random.key(seed), 8)
    inputs = scatter_about(arg_keys[0], (TILES, C, H, W), 1.0, 6.0, ((0, 2), (2, 4), (3, 4)))
    reduce_weight = scatter_about(arg_keys[1], (MID, C), C ** -0.5, 0.375)
    spatial_weight = scatter_about(arg_keys[2], (3, 3, MID, MID), (9 * MID) ** -0.5, 0.25)
    expand_weight = scatter_about(arg_keys[3], (C, MID), MID ** -0.5, 0.75)
    class_weight = scatter_about(arg_keys[4], (3, 3, A * K, C), (9 * C) ** -0.5, 0.125)
    anchor_labels = draw_anchor_labels(jax.random.fold_in(arg_keys[7], 71), 0)
    anchor_mask = draw_anchor_mask(jax.random.fold_in(arg_keys[7], 71), 0)
    return dict(inputs=inputs, reduce_weight=reduce_weight, spatial_weight=spatial_weight, expand_weight=expand_weight, class_weight=class_weight, anchor_labels=anchor_labels, anchor_mask=anchor_mask)


def conv_three(padded, weight, rows, cols):
    total = jnp.zeros((padded.shape[0], weight.shape[2], rows, cols), jnp.float32)
    for dy in range(3):
        for dx in range(3):
            total = total + jnp.einsum('oc,bchw->bohw', weight[dy, dx].astype(jnp.float32), padded[:, :, dy:dy + rows, dx:dx + cols].astype(jnp.float32), precision=lax.Precision.HIGHEST)
    return total

def weight_three(dout, padded, rows, cols):
    taps = []
    for dy in range(3):
        for dx in range(3):
            taps.append(jnp.einsum('bohw,bchw->oc', dout.astype(jnp.float32), padded[:, :, dy:dy + rows, dx:dx + cols].astype(jnp.float32), precision=lax.Precision.HIGHEST))
    return jnp.stack(taps).reshape(3, 3, taps[0].shape[0], taps[0].shape[1])

def input_three(dout_pad, weight, rows, cols):
    total = jnp.zeros((dout_pad.shape[0], weight.shape[3], rows, cols), jnp.float32)
    for ey in range(3):
        for ex in range(3):
            total = total + jnp.einsum('oc,bohw->bchw', weight[2 - ey, 2 - ex].astype(jnp.float32), dout_pad[:, :, ey:ey + rows, ex:ex + cols].astype(jnp.float32), precision=lax.Precision.HIGHEST)
    return total

def focal_terms(logits, labels, mask):
    shaped = logits.reshape(logits.shape[0], A, K, logits.shape[2], logits.shape[3])
    classes = jnp.arange(1, K + 1, dtype=jnp.int32)[None, None, :, None, None]
    target = labels[:, :, None] == classes
    signs = jnp.where(target, 1.0, -1.0).astype(shaped.dtype)
    alpha = jnp.where(target, 0.25, 0.75).astype(shaped.dtype)
    terms = -alpha * jax.nn.sigmoid(-signs * shaped) ** 2 * jax.nn.log_sigmoid(signs * shaped)
    return jnp.sum(terms * mask[:, :, None].astype(shaped.dtype))

def pad_cells(field):
    return jnp.pad(field, ((0, 0), (0, 0), (1, 1), (1, 1)))

def one_tile(inputs, labels, mask, reduce_weight, spatial_weight, expand_weight, class_weight):
    rows, cols = (inputs.shape[2], inputs.shape[3])
    first = jax.nn.relu(jnp.einsum('mc,bchw->bmhw', reduce_weight.astype(jnp.float32), inputs.astype(jnp.float32), precision=lax.Precision.HIGHEST)).astype(jnp.bfloat16)
    first_pad = pad_cells(first)
    second = jax.nn.relu(conv_three(first_pad, spatial_weight, rows, cols)).astype(jnp.bfloat16)
    block = jax.nn.relu(inputs.astype(jnp.float32) + jnp.einsum('cm,bmhw->bchw', expand_weight.astype(jnp.float32), second.astype(jnp.float32), precision=lax.Precision.HIGHEST)).astype(jnp.bfloat16)
    block_pad = pad_cells(block)
    logits = conv_three(block_pad, class_weight, rows, cols)
    focal, pullback = jax.vjp(lambda z: focal_terms(z, labels, mask), logits)
    dlogits = pullback(jnp.ones_like(focal))[0].astype(jnp.bfloat16)
    count = jnp.sum((labels > 0).astype(jnp.float32))
    class_sum = weight_three(dlogits, block_pad, rows, cols)
    dblock = input_three(pad_cells(dlogits), class_weight, rows, cols)
    dsum = jnp.where(block > 0, dblock, 0.0).astype(jnp.bfloat16)
    expand_sum = jnp.einsum('bchw,bmhw->cm', dsum.astype(jnp.float32), second.astype(jnp.float32), precision=lax.Precision.HIGHEST)
    dsecond = jnp.where(second > 0, jnp.einsum('cm,bchw->bmhw', expand_weight.astype(jnp.float32), dsum.astype(jnp.float32), precision=lax.Precision.HIGHEST), 0.0).astype(jnp.bfloat16)
    spatial_sum = weight_three(dsecond, first_pad, rows, cols)
    dfirst = jnp.where(first > 0, input_three(pad_cells(dsecond), spatial_weight, rows, cols), 0.0).astype(jnp.bfloat16)
    reduce_sum = jnp.einsum('bmhw,bchw->mc', dfirst.astype(jnp.float32), inputs.astype(jnp.float32), precision=lax.Precision.HIGHEST)
    return (reduce_sum, spatial_sum, expand_sum, class_sum, focal, count)

def reference(inputs, reduce_weight, spatial_weight, expand_weight, class_weight, anchor_labels, anchor_mask):

    def per_tile(items):
        return one_tile(items[0][None], items[1][None], items[2][None], reduce_weight, spatial_weight, expand_weight, class_weight)
    results = lax.map(per_tile, (inputs, anchor_labels, anchor_mask))
    summed = [lax.optimization_barrier(jnp.sum(item, axis=0)) for item in results]
    positives = summed[5]
    loss = summed[4] / positives
    return (loss, summed[0] / positives, summed[1] / positives, summed[2] / positives, summed[3] / positives)
```

```python
import functools

import jax
import jax.numpy as jnp
import numpy as np
from jax import lax
from jax.experimental import pallas as pl
from jax.experimental.pallas import tpu as pltpu
from jax.sharding import PartitionSpec as P

A = 9
K = 15
GROUP = 4
WIDE = 8
LOG2E = 1.4426950408889634
LN2 = 0.6931471805599453
F32 = jnp.float32
BF16 = jnp.bfloat16
AXES = ("dp", "row", "col")


def dot(a, b):
    return jnp.dot(a, b, preferred_element_type=F32)


def dot_t(a, b):
    return lax.dot_general(a, b, (((1,), (1,)), ((), ())), preferred_element_type=F32)


def step_kernel(
    sizes, heads,
    x_ref, code_ref, spread_ref, wr_ref, ws_ref, wsb_ref, we_ref, wet_ref, wc_ref, wcb_ref,
    pack_ref, stat_ref,
    first, second, block, dlog, dzero, dsec, dsec_zero, acc_c, acc_s, acc_e, acc_r,
    strips, got, ssem, rsem,
):
    rows, chans, cols = x_ref.shape
    mid = wr_ref.shape[0]
    outs = wc_ref.shape[1]
    me = {axis: lax.axis_index(axis) for axis in ("row", "col")}
    mesh_id = pl.DeviceIdType.MESH
    sides = [(axis, step) for axis in ("row", "col") for step in (1, -1)]

    def exists(axis, step):
        return me[axis] < sizes[axis] - 1 if step > 0 else me[axis] > 0

    barrier = pltpu.get_barrier_semaphore()
    for axis, step in sides:
        @pl.when(exists(axis, step))
        def _():
            pl.semaphore_signal(
                barrier, inc=1, device_id={axis: me[axis] + step}, device_id_type=mesh_id
            )

    def push(n, src, dst, axis, step):
        copy = pltpu.make_async_remote_copy(
            src_ref=src, dst_ref=dst, send_sem=ssem.at[n], recv_sem=rsem.at[n],
            device_id={axis: me[axis] + step}, device_id_type=mesh_id,
        )

        @pl.when(exists(axis, step))
        def _():
            copy.start()

        def finish():
            @pl.when(exists(axis, step))
            def _():
                copy.wait_send()

            @pl.when(exists(axis, -step))
            def _():
                copy.wait_recv()

        return finish

    def loop(steps, body, init=0):
        return lax.fori_loop(0, steps, body, init)

    def cat(ref, at, count, low=None, high=None):
        part = slice(low, high)
        return jnp.concatenate([ref[at + k, part, :] for k in range(count)], axis=1)

    def spread_rows(ref, at, value, low=None, high=None):
        for k in range(value.shape[1] // cols):
            ref[at + k, low:high, :] = value[:, k * cols:(k + 1) * cols]

    def clear_edges(n, field, depth):
        blank = jnp.zeros((depth, cols), BF16)

        @pl.when(jnp.logical_not(exists("row", -1)))
        def _():
            field[0, depth:2 * depth, :] = blank

        @pl.when(jnp.logical_not(exists("row", 1)))
        def _():
            field[rows + 1, depth:2 * depth, :] = blank

        for side in range(2):
            @pl.when(jnp.logical_not(exists("col", 1 if side else -1)))
            def _():
                got[n][side] = blank

    def send_rows(n, field, depth):
        down = push(
            4 * n, field.at[rows, pl.ds(depth, depth)], field.at[0, pl.ds(depth, depth)], "row", 1
        )
        up = push(
            4 * n + 1, field.at[1, pl.ds(depth, depth)],
            field.at[rows + 1, pl.ds(depth, depth)], "row", -1,
        )
        return down, up

    def send_strip(n, field, depth, held):
        lane = lax.broadcasted_iota(jnp.int32, (depth, cols), 1)

        def gather(i, strip):
            row = field[i, depth:2 * depth, :]
            return jnp.where(lane // 2 == i, pltpu.roll(row, 2 * i + 1, 1), strip)

        strip = lax.fori_loop(1, rows + 1, gather, jnp.zeros((depth, cols), BF16))
        for wait in held:
            wait()
        strip = gather(rows + 1, gather(0, strip))
        strips[n][...] = strip
        right = push(4 * n + 2, strips[n], got[n].at[0], "col", 1)
        left = push(4 * n + 3, strips[n], got[n].at[1], "col", -1)
        return right, left

    def widen(n, field, depth, held):
        for wait in held:
            wait()
        lane = lax.broadcasted_iota(jnp.int32, (depth, cols), 1)
        before, after = got[n][0], got[n][1]

        def fill(i, c):
            row = field[i, depth:2 * depth, :]
            field[i, :depth, :] = jnp.where(
                lane == 0, pltpu.roll(before, cols - 2 * i, 1), pltpu.roll(row, 1, 1)
            )
            field[i, 2 * depth:, :] = jnp.where(
                lane == cols - 1, pltpu.roll(after, cols - 2 - 2 * i, 1),
                pltpu.roll(row, cols - 1, 1),
            )
            return c

        loop(rows + 2, fill)

    def conv(weight, field, at):
        return sum(dot(weight[dy], cat(field, at + dy, GROUP)) for dy in range(3))

    fields = [(first, mid), (block, chans), (dlog, outs), (dsec, mid)]
    for n, (field, depth) in enumerate(fields):
        clear_edges(n, field, depth)
    for ref in (dzero, dsec_zero):
        ref[0] = jnp.zeros(ref.shape[1:], BF16)
        ref[rows + 1] = jnp.zeros(ref.shape[1:], BF16)
    for ref in (acc_c, acc_s, acc_e, acc_r):
        ref[...] = jnp.zeros_like(ref)
    peers = sum(jnp.where(exists(axis, step), 1, 0) for axis, step in sides)
    pl.semaphore_wait(barrier, peers)

    def make_first(i, c):
        z = dot(wr_ref[...], cat(x_ref, i * GROUP, GROUP))
        spread_rows(first, i * GROUP + 1, jnp.maximum(z, 0.0).astype(BF16), mid, 2 * mid)
        return c

    loop(rows // GROUP, make_first)
    held = send_rows(0, first, mid)
    held = send_strip(0, first, mid, held)
    widen(0, first, mid, held)

    def make_block(i, c):
        s = jnp.maximum(conv(ws_ref, first, i * GROUP), 0.0).astype(BF16)
        spread_rows(second, i * GROUP, s)
        b = jnp.maximum(cat(x_ref, i * GROUP, GROUP).astype(F32) + dot(we_ref[...], s), 0.0)
        spread_rows(block, i * GROUP + 1, b.astype(BF16), chans, 2 * chans)
        return c

    loop(rows // GROUP, make_block)
    held = send_rows(1, block, chans)
    held = send_strip(1, block, chans, held)
    widen(1, block, chans, held)

    def make_dlog(i, carry):
        total, count = carry
        z = conv(wc_ref, block, i * GROUP)
        code = cat(code_ref, i * GROUP, GROUP)
        gap = dot(spread_ref[...], code)
        target = gap == 0.0
        alpha = jnp.where(target, 0.25, jnp.where(gap > 32.0, 0.0, 0.75))
        z = z * LOG2E
        u = jnp.where(target, -z, z)
        e = jnp.exp2(-jnp.abs(u))
        soft = jnp.maximum(u, 0.0) + jnp.log2(1.0 + e)
        prob = jnp.exp2(u - soft)
        scaled = alpha * prob * prob
        total = total + jnp.sum(scaled * soft, axis=0, keepdims=True)
        slope = scaled * ((2.0 * LN2 - 2.0 * LN2 * prob) * soft + prob)
        d = jnp.where(target, -slope, slope).astype(BF16)
        spread_rows(dlog, i * GROUP + 1, d, outs, 2 * outs)
        spread_rows(dzero, i * GROUP + 1, d)
        codes = code.astype(F32)
        row = lax.broadcasted_iota(jnp.int32, codes.shape, 0)
        hit = jnp.where((codes > 0.5) & (codes < 32.0) & (row < A), 1.0, 0.0)
        count = count + jnp.sum(hit, axis=0, keepdims=True)
        return total, count

    zero = jnp.zeros((1, GROUP * cols), F32)
    total, count = loop(rows // GROUP, make_dlog, (zero, zero))
    fold = lambda v: sum(v[:, k * 128:(k + 1) * 128] for k in range(v.shape[1] // 128))
    stat_ref[0:1, :] = fold(total) * LN2
    stat_ref[1:2, :] = fold(count)
    stat_ref[2:, :] = jnp.zeros((6, 128), F32)
    held = send_rows(2, dlog, outs)

    def weight_sum(acc, grad, field):
        depth = grad.shape[1]

        def add(i, c):
            at = i * WIDE + 1
            tall = jnp.concatenate([cat(grad, at + 1 - dy, WIDE) for dy in range(3)], axis=0)
            acc[...] += dot_t(tall, cat(field, at, WIDE))
            return c

        loop(rows // WIDE, add)
        acc[:depth, :] += dot_t(grad[1], field[0])
        acc[2 * depth:, :] += dot_t(grad[rows], field[rows + 1])

    weight_sum(acc_c, dzero, block)
    held = send_strip(2, dlog, outs, held)
    widen(2, dlog, outs, held)

    def make_dsec(i, c):
        g = conv(wcb_ref, dlog, i * GROUP)
        b = cat(block, i * GROUP + 1, GROUP, chans, 2 * chans).astype(F32)
        ds = jnp.where(b > 0.0, g, 0.0).astype(BF16)
        s = cat(second, i * GROUP, GROUP)
        acc_e[...] += dot_t(s, ds)
        h = dot(wet_ref[...], ds)
        d = jnp.where(s.astype(F32) > 0.0, h, 0.0).astype(BF16)
        spread_rows(dsec, i * GROUP + 1, d, mid, 2 * mid)
        spread_rows(dsec_zero, i * GROUP + 1, d)
        return c

    loop(rows // GROUP, make_dsec)
    held = send_rows(3, dsec, mid)
    weight_sum(acc_s, dsec_zero, first)
    held = send_strip(3, dsec, mid, held)
    widen(3, dsec, mid, held)

    def make_dfirst(i, c):
        g = conv(wsb_ref, dsec, i * GROUP)
        f = cat(first, i * GROUP + 1, GROUP, mid, 2 * mid).astype(F32)
        df = jnp.where(f > 0.0, g, 0.0).astype(BF16)
        acc_r[...] += dot_t(df, cat(x_ref, i * GROUP, GROUP))
        return c

    loop(rows // GROUP, make_dfirst)
    spots = layout(mid, heads)[:3]
    pack_ref[9 * heads:, :] = jnp.zeros((pack_ref.shape[0] - 9 * heads, chans), F32)
    for dy in range(3):
        for dx in range(3):
            tap = 3 * dy + dx
            pack_ref[tap * heads:(tap + 1) * heads, :] = acc_c[
                dy * outs:dy * outs + heads, dx * chans:(dx + 1) * chans
            ]
    pack_ref[spots[0]:spots[0] + mid, :] = acc_r[...]
    pack_ref[spots[1]:spots[1] + mid, :] = acc_e[...]
    pack_ref[spots[2]:spots[2] + 3 * mid, :3 * mid] = acc_s[...]


def layout(mid, heads):
    first = -(-9 * heads // 8) * 8
    return first, first + mid, first + 2 * mid, first + 5 * mid


def piece_rows(s, orders, sizes, total):
    rows, out = total // len(orders), []
    for axis in orders[s]:
        rows //= sizes[axis]
        out.append(rows)
    return out


def sum_kernel(sizes, orders, pack_ref, stat_ref, out_ref, total_ref, *scratch):
    subs, depth = len(orders), len(AXES)
    send, full = scratch[0], scratch[1]
    recvs = [scratch[2 + s * depth:2 + (s + 1) * depth] for s in range(subs)]
    stat_send = scratch[2 + subs * depth]
    stat_recv = scratch[3 + subs * depth:3 + subs * depth + depth]
    ssem, rsem = scratch[-2:]
    total = pack_ref.shape[0]
    share = total // subs
    me = {axis: lax.axis_index(axis) for axis in AXES}
    peers = lambda axis: range(1, sizes[axis])
    mesh_id = pl.DeviceIdType.MESH

    barrier = pltpu.get_barrier_semaphore()
    for axis in AXES:
        for d in peers(axis):
            pl.semaphore_signal(
                barrier, inc=1, device_id={axis: lax.rem(me[axis] + d, sizes[axis])},
                device_id_type=mesh_id,
            )
    pl.semaphore_wait(barrier, sum(sizes[axis] - 1 for axis in AXES))

    used = [0]

    def push(src, dst, axis, d):
        n = used[0]
        used[0] += 1
        copy = pltpu.make_async_remote_copy(
            src_ref=src, dst_ref=dst, send_sem=ssem.at[n], recv_sem=rsem.at[n],
            device_id={axis: lax.rem(me[axis] + d, sizes[axis])}, device_id_type=mesh_id,
        )
        copy.start()
        return copy

    send[...] = pack_ref[...].astype(BF16)
    base = [s * share for s in range(subs)]
    held = [None] * subs
    stat = stat_ref[...]
    for k in range(depth):
        copies = []
        for s in range(subs):
            axis = orders[s][k]
            rows = piece_rows(s, orders, sizes, total)[k]
            for d in peers(axis):
                to = lax.rem(me[axis] + d, sizes[axis])
                src = send.at[pl.ds(pl.multiple_of(base[s] + to * rows, 16), rows)]
                copies.append(push(src, recvs[s][k].at[d - 1], axis, d))
        stat_send[k] = stat
        for d in peers(AXES[k]):
            copies.append(push(stat_send.at[k], stat_recv[k].at[d - 1], AXES[k], d))
        for copy in copies:
            copy.wait()
        for d in peers(AXES[k]):
            stat = stat + stat_recv[k][d - 1]
        for s in range(subs):
            axis = orders[s][k]
            rows = piece_rows(s, orders, sizes, total)[k]
            mine = me[axis] * rows
            if k == 0:
                got = pack_ref[pl.ds(pl.multiple_of(base[s] + mine, 16), rows), :]
            else:
                out_at = pl.ds(pl.multiple_of(base[s] + mine, 16), rows)
                got = out_ref[out_at, :]
            for d in peers(axis):
                got = got + recvs[s][k][d - 1].astype(F32)
            base[s] = pl.multiple_of(base[s] + mine, 16)
            where = pl.ds(base[s], rows)
            if k < depth - 1:
                out_ref[where, :] = got
                send[where, :] = got.astype(BF16)
            else:
                full[where, :] = got.astype(BF16)
    total_ref[...] = stat
    for k in range(depth - 1, -1, -1):
        copies = []
        for s in range(subs):
            axis = orders[s][k]
            rows = piece_rows(s, orders, sizes, total)[k]
            where = pl.ds(base[s], rows)
            for d in peers(axis):
                copies.append(push(full.at[where], full.at[where], axis, d))
            base[s] = pl.multiple_of(base[s] - me[axis] * rows, 16)
        for copy in copies:
            copy.wait()
    out_ref[...] = full[...].astype(F32)


def sum_devices(pack, stat):
    sizes = {axis: lax.axis_size(axis) for axis in AXES}
    orders = [AXES[s:] + AXES[:s] for s in range(len(AXES))]
    total, chans = pack.shape
    scratch = [pltpu.VMEM((total, chans), BF16), pltpu.VMEM((total, chans), BF16)]
    copies = 0
    for s in range(len(orders)):
        for axis, rows in zip(orders[s], piece_rows(s, orders, sizes, total)):
            scratch.append(pltpu.VMEM((max(sizes[axis] - 1, 1), rows, chans), BF16))
            copies += 2 * (sizes[axis] - 1)
    scratch.append(pltpu.VMEM((len(AXES),) + stat.shape, F32))
    for axis in AXES:
        scratch.append(pltpu.VMEM((max(sizes[axis] - 1, 1),) + stat.shape, F32))
        copies += sizes[axis] - 1
    scratch += [pltpu.SemaphoreType.DMA((copies,)), pltpu.SemaphoreType.DMA((copies,))]
    return pl.pallas_call(
        functools.partial(sum_kernel, sizes, orders),
        out_shape=(
            jax.ShapeDtypeStruct(pack.shape, F32), jax.ShapeDtypeStruct(stat.shape, F32)
        ),
        in_specs=[pl.BlockSpec(memory_space=pltpu.VMEM)] * 2,
        out_specs=[pl.BlockSpec(memory_space=pltpu.VMEM)] * 2,
        scratch_shapes=scratch,
        compiler_params=pltpu.CompilerParams(
            collective_id=0, has_side_effects=True, vmem_limit_bytes=16 * 1024 * 1024
        ),
        name="sum_devices",
    )(pack, stat)


def per_device(
    inputs, reduce_weight, spatial_weight, expand_weight, class_weight, anchor_labels, anchor_mask
):
    tiles, chans, rows, cols = inputs.shape
    assert tiles == 1
    mid = reduce_weight.shape[0]
    heads = class_weight.shape[2]
    outs = -(-heads // 16) * 16
    sizes = {axis: lax.axis_size(axis) for axis in ("row", "col")}

    code = jnp.where(anchor_mask[0] > 0, anchor_labels[0], 64).astype(BF16)
    code = jnp.concatenate([
        code, jnp.ones((1, rows, cols), BF16), jnp.zeros((16 - A - 1, rows, cols), BF16)
    ], axis=0).transpose(1, 0, 2)
    x = inputs[0].transpose(1, 0, 2)

    spread = np.zeros((outs, 16), np.float32)
    spread[np.arange(heads), np.arange(heads) // K] = 1.0
    spread[np.arange(heads), A] = -1.0 - np.arange(heads) % K
    spread[heads:, A] = 64.0
    spread = jnp.asarray(spread, BF16)

    flip = lambda w: w[::-1, ::-1].transpose(0, 3, 1, 2)
    wide = jnp.pad(class_weight, ((0, 0), (0, 0), (0, outs - heads), (0, 0)))
    ws = spatial_weight.transpose(0, 2, 1, 3).reshape(3, mid, 3 * mid)
    wsb = flip(spatial_weight).reshape(3, mid, 3 * mid)
    wc = wide.transpose(0, 2, 1, 3).reshape(3, outs, 3 * chans)
    wcb = flip(wide).reshape(3, chans, 3 * outs)

    unit = 16 * len(AXES) * int(np.prod([lax.axis_size(axis) for axis in AXES]))
    packed = -(-layout(mid, heads)[3] // unit) * unit
    depths = (mid, chans, outs, mid)

    sums = pl.pallas_call(
        functools.partial(step_kernel, sizes, heads),
        out_shape=(
            jax.ShapeDtypeStruct((packed, chans), F32),
            jax.ShapeDtypeStruct((8, 128), F32),
        ),
        in_specs=[pl.BlockSpec(memory_space=pltpu.VMEM)] * 10,
        out_specs=[pl.BlockSpec(memory_space=pltpu.VMEM)] * 2,
        scratch_shapes=[
            pltpu.VMEM((rows + 2, 3 * mid, cols), BF16),
            pltpu.VMEM((rows, mid, cols), BF16),
            pltpu.VMEM((rows + 2, 3 * chans, cols), BF16),
            pltpu.VMEM((rows + 2, 3 * outs, cols), BF16),
            pltpu.VMEM((rows + 2, outs, cols), BF16),
            pltpu.VMEM((rows + 2, 3 * mid, cols), BF16),
            pltpu.VMEM((rows + 2, mid, cols), BF16),
            pltpu.VMEM((3 * outs, 3 * chans), F32),
            pltpu.VMEM((3 * mid, 3 * mid), F32),
            pltpu.VMEM((mid, chans), F32),
            pltpu.VMEM((mid, chans), F32),
            [pltpu.VMEM((depth, cols), BF16) for depth in depths],
            [pltpu.VMEM((2, depth, cols), BF16) for depth in depths],
            pltpu.SemaphoreType.DMA((16,)),
            pltpu.SemaphoreType.DMA((16,)),
        ],
        compiler_params=pltpu.CompilerParams(
            collective_id=1, has_side_effects=True, vmem_limit_bytes=56 * 1024 * 1024
        ),
        name="tile_step",
    )(x, code, spread, reduce_weight, ws, wsb, expand_weight, expand_weight.T, wc, wcb)
    return finish(sums, mid, heads)


def finish(sums, mid, heads):
    pack, stat = sum_devices(*sums)
    chans = pack.shape[1]
    spots = layout(mid, heads)
    count = jnp.sum(stat[1])
    scale = 1.0 / count
    spatial = pack[spots[2]:spots[3], :3 * mid].reshape(3, mid, 3, mid).transpose(0, 2, 1, 3)
    return (
        jnp.sum(stat[0]) / count,
        pack[spots[0]:spots[1]] * scale,
        spatial * scale,
        pack[spots[1]:spots[2]].T * scale,
        pack[:9 * heads].reshape(3, 3, heads, chans) * scale,
    )


def solution(mesh):
    tiled = P("dp", None, "row", "col")
    return jax.shard_map(
        per_device,
        mesh=mesh,
        in_specs=(tiled, P(), P(), P(), P(), tiled, tiled),
        out_specs=(P(), P(), P(), P(), P()),
        check_vma=False,
    )
```

```python
import functools

import jax
import jax.numpy as jnp
import numpy as np
from jax import lax
from jax.experimental import pallas as pl
from jax.experimental.pallas import tpu as pltpu
from jax.sharding import PartitionSpec as P

A = 9
K = 15
GROUP = 4
WIDE = 8
LOG2E = 1.4426950408889634
LN2 = 0.6931471805599453
F32 = jnp.float32
BF16 = jnp.bfloat16
AXES = ("dp", "row", "col")


def dot(a, b):
    return jnp.dot(a, b, preferred_element_type=F32)


def dot_t(a, b):
    return lax.dot_general(a, b, (((1,), (1,)), ((), ())), preferred_element_type=F32)


def step_kernel(
    sizes, heads,
    x_ref, label_ref, mask_ref, spread_ref, wr_ref, spatial_ref, we_ref, class_ref,
    pack_ref, stat_ref,
    first, second, block, dlog, dzero, dsec, dsec_zero, acc_c, acc_s, acc_e, acc_r,
    code_ref, ws_ref, wsb_ref, wet_ref, wc_ref, wcb_ref, strips, got, ssem, rsem,
):
    rows, chans, cols = x_ref.shape
    mid = wr_ref.shape[0]
    outs = wc_ref.shape[2]
    me = {axis: lax.axis_index(axis) for axis in ("row", "col")}
    mesh_id = pl.DeviceIdType.MESH
    sides = [(axis, step) for axis in ("row", "col") for step in (1, -1)]

    def exists(axis, step):
        return me[axis] < sizes[axis] - 1 if step > 0 else me[axis] > 0

    barrier = pltpu.get_barrier_semaphore()
    for axis, step in sides:
        @pl.when(exists(axis, step))
        def _():
            pl.semaphore_signal(
                barrier, inc=1, device_id={axis: me[axis] + step}, device_id_type=mesh_id
            )

    def push(n, src, dst, axis, step):
        copy = pltpu.make_async_remote_copy(
            src_ref=src, dst_ref=dst, send_sem=ssem.at[n], recv_sem=rsem.at[n],
            device_id={axis: me[axis] + step}, device_id_type=mesh_id,
        )

        @pl.when(exists(axis, step))
        def _():
            copy.start()

        def finish():
            @pl.when(exists(axis, step))
            def _():
                copy.wait_send()

            @pl.when(exists(axis, -step))
            def _():
                copy.wait_recv()

        return finish

    def loop(steps, body, init=0):
        return lax.fori_loop(0, steps, body, init)

    def cat(ref, at, count, low=None, high=None):
        part = slice(low, high)
        return jnp.concatenate([ref[at + k, part, :] for k in range(count)], axis=1)

    def spread_rows(ref, at, value, low=None, high=None):
        for k in range(value.shape[1] // cols):
            ref[at + k, low:high, :] = value[:, k * cols:(k + 1) * cols]

    def clear_edges(n, field, depth):
        blank = jnp.zeros((depth, cols), BF16)

        @pl.when(jnp.logical_not(exists("row", -1)))
        def _():
            field[0, depth:2 * depth, :] = blank

        @pl.when(jnp.logical_not(exists("row", 1)))
        def _():
            field[rows + 1, depth:2 * depth, :] = blank

        for side in range(2):
            @pl.when(jnp.logical_not(exists("col", 1 if side else -1)))
            def _():
                got[n][side] = blank

    def send_rows(n, field, depth):
        down = push(
            4 * n, field.at[rows, pl.ds(depth, depth)], field.at[0, pl.ds(depth, depth)], "row", 1
        )
        up = push(
            4 * n + 1, field.at[1, pl.ds(depth, depth)],
            field.at[rows + 1, pl.ds(depth, depth)], "row", -1,
        )
        return down, up

    def publish(n, field, depth, at, value):
        lane = lax.broadcasted_iota(jnp.int32, (depth, cols), 1) // 2
        for k in range(value.shape[1] // cols):
            row = value[:, k * cols:(k + 1) * cols]
            i = at + k
            field[i, depth:2 * depth, :] = row
            field[i, :depth, :] = pltpu.roll(row, 1, 1)
            field[i, 2 * depth:, :] = pltpu.roll(row, cols - 1, 1)
            strips[n][...] = jnp.where(lane == i, pltpu.roll(row, 2 * i + 1, 1), strips[n][...])

    def send_strip(n, field, depth, held):
        for wait in held:
            wait()
        for i in (0, rows + 1):
            publish(n, field, depth, i, field[i, depth:2 * depth, :])
        right = push(4 * n + 2, strips[n], got[n].at[0], "col", 1)
        left = push(4 * n + 3, strips[n], got[n].at[1], "col", -1)
        return right, left

    def widen(n, field, depth, held):
        for wait in held:
            wait()
        lane = lax.broadcasted_iota(jnp.int32, (depth, cols), 1)
        before, after = got[n][0], got[n][1]
        for i in range(rows + 2):
            field[i, :depth, :] = jnp.where(
                lane == 0, pltpu.roll(before, (cols - 2 * i) % cols, 1), field[i, :depth, :]
            )
            field[i, 2 * depth:, :] = jnp.where(
                lane == cols - 1, pltpu.roll(after, (cols - 2 - 2 * i) % cols, 1),
                field[i, 2 * depth:, :],
            )

    def conv(weight, field, at):
        return sum(dot(weight(dy), cat(field, at + dy, GROUP)) for dy in range(3))

    def sweep(body, between, init=0):
        groups = rows // GROUP
        carry = loop(2, lambda j, c: body(j * (groups - 1), c), init)
        held = between()
        return held, loop(groups - 2, lambda j, c: body(j + 1, c), carry)

    fields = [(first, mid), (block, chans), (dlog, outs), (dsec, mid)]
    for n, (field, depth) in enumerate(fields):
        clear_edges(n, field, depth)
        strips[n][...] = jnp.zeros((depth, cols), BF16)
    for ref in (dzero, dsec_zero):
        ref[0] = jnp.zeros(ref.shape[1:], BF16)
        ref[rows + 1] = jnp.zeros(ref.shape[1:], BF16)
    for ref in (acc_c, acc_s, acc_e, acc_r):
        ref[...] = jnp.zeros_like(ref)
    peers = sum(jnp.where(exists(axis, step), 1, 0) for axis, step in sides)
    pl.semaphore_wait(barrier, peers)

    def make_first(i, c):
        z = dot(wr_ref[...], cat(x_ref, i * GROUP, GROUP))
        publish(0, first, mid, i * GROUP + 1, jnp.maximum(z, 0.0).astype(BF16))
        return c

    held, _ = sweep(make_first, lambda: send_rows(0, first, mid))
    for dy in range(3):
        for dx in range(3):
            ws_ref[dy, :, dx * mid:(dx + 1) * mid] = spatial_ref[dy, dx]
            wc_ref[dy, dx, :heads, :] = class_ref[dy, dx]
            wc_ref[dy, dx, heads:, :] = jnp.zeros((outs - heads, chans), BF16)
    for h in range(rows):
        code = jnp.where(mask_ref[:, h, :] > 0, label_ref[:, h, :], 64)
        code_ref[h, :A, :] = code.astype(F32).astype(BF16)
        code_ref[h, A:, :] = jnp.ones((16 - A, cols), BF16)
    held = send_strip(0, first, mid, held)

    def turned(parts):
        size = parts[0].shape[1]
        eye = jnp.where(
            lax.broadcasted_iota(jnp.int32, (size, size), 0)
            == lax.broadcasted_iota(jnp.int32, (size, size), 1), 1.0, 0.0,
        ).astype(BF16)
        return dot_t(eye, jnp.concatenate(parts, axis=0)).astype(BF16)

    wet_ref[...] = turned([we_ref[...]])
    for dy in range(3):
        wsb_ref[dy] = turned([spatial_ref[2 - dy, 2 - dx] for dx in range(3)])
        wcb_ref[dy] = turned([wc_ref[2 - dy, 2 - dx] for dx in range(3)])
    widen(0, first, mid, held)

    def make_block(i, c):
        s = jnp.maximum(conv(lambda dy: ws_ref[dy], first, i * GROUP), 0.0).astype(BF16)
        spread_rows(second, i * GROUP, s)
        b = jnp.maximum(cat(x_ref, i * GROUP, GROUP).astype(F32) + dot(we_ref[...], s), 0.0)
        publish(1, block, chans, i * GROUP + 1, b.astype(BF16))
        return c

    held, _ = sweep(make_block, lambda: send_rows(1, block, chans))
    held = send_strip(1, block, chans, held)
    widen(1, block, chans, held)

    def class_rows(dy):
        return jnp.concatenate([wc_ref[dy, dx] for dx in range(3)], axis=1)

    def make_dlog(i, carry):
        total, count = carry
        z = conv(class_rows, block, i * GROUP)
        code = cat(code_ref, i * GROUP, GROUP)
        gap = dot(spread_ref[...], code)
        target = gap == 0.0
        alpha = jnp.where(target, 0.25, jnp.where(gap > 32.0, 0.0, 0.75))
        z = z * LOG2E
        u = jnp.where(target, -z, z)
        e = jnp.exp2(-jnp.abs(u))
        soft = jnp.maximum(u, 0.0) + jnp.log2(1.0 + e)
        prob = jnp.exp2(u - soft)
        scaled = alpha * prob * prob
        total = total + jnp.sum(scaled * soft, axis=0, keepdims=True)
        slope = scaled * ((2.0 * LN2 - 2.0 * LN2 * prob) * soft + prob)
        d = jnp.where(target, -slope, slope).astype(BF16)
        publish(2, dlog, outs, i * GROUP + 1, d)
        spread_rows(dzero, i * GROUP + 1, d)
        codes = code.astype(F32)
        row = lax.broadcasted_iota(jnp.int32, codes.shape, 0)
        hit = jnp.where((codes > 0.5) & (codes < 32.0) & (row < A), 1.0, 0.0)
        count = count + jnp.sum(hit, axis=0, keepdims=True)
        return total, count

    zero = jnp.zeros((1, GROUP * cols), F32)
    held, (total, count) = sweep(make_dlog, lambda: send_rows(2, dlog, outs), (zero, zero))
    fold = lambda v: sum(v[:, k * 128:(k + 1) * 128] for k in range(v.shape[1] // 128))
    stat_ref[0:1, :] = fold(total) * LN2
    stat_ref[1:2, :] = fold(count)
    stat_ref[2:, :] = jnp.zeros((6, 128), F32)

    def weight_sum(acc, grad, field):
        depth = grad.shape[1]

        def add(i, c):
            at = i * WIDE + 1
            tall = jnp.concatenate([cat(grad, at + 1 - dy, WIDE) for dy in range(3)], axis=0)
            acc[...] += dot_t(tall, cat(field, at, WIDE))
            return c

        loop(rows // WIDE, add)
        acc[:depth, :] += dot_t(grad[1], field[0])
        acc[2 * depth:, :] += dot_t(grad[rows], field[rows + 1])

    weight_sum(acc_c, dzero, block)
    held = send_strip(2, dlog, outs, held)
    widen(2, dlog, outs, held)

    def make_dsec(i, c):
        g = conv(lambda dy: wcb_ref[dy], dlog, i * GROUP)
        b = cat(block, i * GROUP + 1, GROUP, chans, 2 * chans).astype(F32)
        ds = jnp.where(b > 0.0, g, 0.0).astype(BF16)
        s = cat(second, i * GROUP, GROUP)
        acc_e[...] += dot_t(s, ds)
        h = dot(wet_ref[...], ds)
        d = jnp.where(s.astype(F32) > 0.0, h, 0.0).astype(BF16)
        publish(3, dsec, mid, i * GROUP + 1, d)
        spread_rows(dsec_zero, i * GROUP + 1, d)
        return c

    held, _ = sweep(make_dsec, lambda: send_rows(3, dsec, mid))
    weight_sum(acc_s, dsec_zero, first)
    held = send_strip(3, dsec, mid, held)
    widen(3, dsec, mid, held)

    def make_dfirst(i, c):
        g = conv(lambda dy: wsb_ref[dy], dsec, i * GROUP)
        f = cat(first, i * GROUP + 1, GROUP, mid, 2 * mid).astype(F32)
        df = jnp.where(f > 0.0, g, 0.0).astype(BF16)
        acc_r[...] += dot_t(df, cat(x_ref, i * GROUP, GROUP))
        return c

    loop(rows // GROUP, make_dfirst)
    spots = layout(mid, heads)[:3]
    pack_ref[9 * heads:, :] = jnp.zeros((pack_ref.shape[0] - 9 * heads, chans), F32)
    for dy in range(3):
        for dx in range(3):
            tap = 3 * dy + dx
            pack_ref[tap * heads:(tap + 1) * heads, :] = acc_c[
                dy * outs:dy * outs + heads, dx * chans:(dx + 1) * chans
            ]
    pack_ref[spots[0]:spots[0] + mid, :] = acc_r[...]
    pack_ref[spots[1]:spots[1] + mid, :] = acc_e[...]
    pack_ref[spots[2]:spots[2] + 3 * mid, :3 * mid] = acc_s[...]


def layout(mid, heads):
    first = -(-9 * heads // 8) * 8
    return first, first + mid, first + 2 * mid, first + 5 * mid


def piece_rows(s, orders, sizes, total):
    rows, out = total // len(orders), []
    for axis in orders[s]:
        rows //= sizes[axis]
        out.append(rows)
    return out


def sum_kernel(sizes, orders, pack_ref, stat_ref, out_ref, total_ref, *scratch):
    subs, depth = len(orders), len(AXES)
    send, full = scratch[0], scratch[1]
    recvs = [scratch[2 + s * depth:2 + (s + 1) * depth] for s in range(subs)]
    stat_send = scratch[2 + subs * depth]
    stat_recv = scratch[3 + subs * depth:3 + subs * depth + depth]
    ssem, rsem = scratch[-2:]
    total = pack_ref.shape[0]
    share = total // subs
    me = {axis: lax.axis_index(axis) for axis in AXES}
    peers = lambda axis: range(1, sizes[axis])
    mesh_id = pl.DeviceIdType.MESH

    barrier = pltpu.get_barrier_semaphore()
    for axis in AXES:
        for d in peers(axis):
            pl.semaphore_signal(
                barrier, inc=1, device_id={axis: lax.rem(me[axis] + d, sizes[axis])},
                device_id_type=mesh_id,
            )
    pl.semaphore_wait(barrier, sum(sizes[axis] - 1 for axis in AXES))

    used = [0]

    def push(src, dst, axis, d):
        n = used[0]
        used[0] += 1
        copy = pltpu.make_async_remote_copy(
            src_ref=src, dst_ref=dst, send_sem=ssem.at[n], recv_sem=rsem.at[n],
            device_id={axis: lax.rem(me[axis] + d, sizes[axis])}, device_id_type=mesh_id,
        )
        copy.start()
        return copy

    send[...] = pack_ref[...].astype(BF16)
    base = [s * share for s in range(subs)]
    held = [None] * subs
    stat = stat_ref[...]
    for k in range(depth):
        copies = []
        for s in range(subs):
            axis = orders[s][k]
            rows = piece_rows(s, orders, sizes, total)[k]
            for d in peers(axis):
                to = lax.rem(me[axis] + d, sizes[axis])
                src = send.at[pl.ds(pl.multiple_of(base[s] + to * rows, 16), rows)]
                copies.append(push(src, recvs[s][k].at[d - 1], axis, d))
        stat_send[k] = stat
        for d in peers(AXES[k]):
            copies.append(push(stat_send.at[k], stat_recv[k].at[d - 1], AXES[k], d))
        for copy in copies:
            copy.wait()
        for d in peers(AXES[k]):
            stat = stat + stat_recv[k][d - 1]
        for s in range(subs):
            axis = orders[s][k]
            rows = piece_rows(s, orders, sizes, total)[k]
            mine = me[axis] * rows
            if k == 0:
                got = pack_ref[pl.ds(pl.multiple_of(base[s] + mine, 16), rows), :]
            else:
                out_at = pl.ds(pl.multiple_of(base[s] + mine, 16), rows)
                got = out_ref[out_at, :]
            for d in peers(axis):
                got = got + recvs[s][k][d - 1].astype(F32)
            base[s] = pl.multiple_of(base[s] + mine, 16)
            where = pl.ds(base[s], rows)
            if k < depth - 1:
                out_ref[where, :] = got
                send[where, :] = got.astype(BF16)
            else:
                full[where, :] = got.astype(BF16)
    total_ref[...] = stat
    for k in range(depth - 1, -1, -1):
        copies = []
        for s in range(subs):
            axis = orders[s][k]
            rows = piece_rows(s, orders, sizes, total)[k]
            where = pl.ds(base[s], rows)
            for d in peers(axis):
                copies.append(push(full.at[where], full.at[where], axis, d))
            base[s] = pl.multiple_of(base[s] - me[axis] * rows, 16)
        for copy in copies:
            copy.wait()
    out_ref[...] = full[...].astype(F32)


def sum_devices(pack, stat):
    sizes = {axis: lax.axis_size(axis) for axis in AXES}
    orders = [AXES[s:] + AXES[:s] for s in range(len(AXES))]
    total, chans = pack.shape
    scratch = [pltpu.VMEM((total, chans), BF16), pltpu.VMEM((total, chans), BF16)]
    copies = 0
    for s in range(len(orders)):
        for axis, rows in zip(orders[s], piece_rows(s, orders, sizes, total)):
            scratch.append(pltpu.VMEM((max(sizes[axis] - 1, 1), rows, chans), BF16))
            copies += 2 * (sizes[axis] - 1)
    scratch.append(pltpu.VMEM((len(AXES),) + stat.shape, F32))
    for axis in AXES:
        scratch.append(pltpu.VMEM((max(sizes[axis] - 1, 1),) + stat.shape, F32))
        copies += sizes[axis] - 1
    scratch += [pltpu.SemaphoreType.DMA((copies,)), pltpu.SemaphoreType.DMA((copies,))]
    return pl.pallas_call(
        functools.partial(sum_kernel, sizes, orders),
        out_shape=(
            jax.ShapeDtypeStruct(pack.shape, F32), jax.ShapeDtypeStruct(stat.shape, F32)
        ),
        in_specs=[pl.BlockSpec(memory_space=pltpu.VMEM)] * 2,
        out_specs=[pl.BlockSpec(memory_space=pltpu.VMEM)] * 2,
        scratch_shapes=scratch,
        compiler_params=pltpu.CompilerParams(
            collective_id=0, has_side_effects=True, vmem_limit_bytes=16 * 1024 * 1024
        ),
        name="sum_devices",
    )(pack, stat)


def per_device(
    inputs, reduce_weight, spatial_weight, expand_weight, class_weight, anchor_labels, anchor_mask
):
    tiles, chans, rows, cols = inputs.shape
    assert tiles == 1
    mid = reduce_weight.shape[0]
    heads = class_weight.shape[2]
    outs = -(-heads // 16) * 16
    sizes = {axis: lax.axis_size(axis) for axis in ("row", "col")}

    x = inputs[0].transpose(1, 0, 2)

    spread = np.zeros((outs, 16), np.float32)
    spread[np.arange(heads), np.arange(heads) // K] = 1.0
    spread[np.arange(heads), A] = -1.0 - np.arange(heads) % K
    spread[heads:, A] = 64.0
    spread = jnp.asarray(spread, BF16)

    unit = 16 * len(AXES) * int(np.prod([lax.axis_size(axis) for axis in AXES]))
    packed = -(-layout(mid, heads)[3] // unit) * unit
    depths = (mid, chans, outs, mid)

    sums = pl.pallas_call(
        functools.partial(step_kernel, sizes, heads),
        out_shape=(
            jax.ShapeDtypeStruct((packed, chans), F32),
            jax.ShapeDtypeStruct((8, 128), F32),
        ),
        in_specs=[pl.BlockSpec(memory_space=pltpu.VMEM)] * 8,
        out_specs=[pl.BlockSpec(memory_space=pltpu.VMEM)] * 2,
        scratch_shapes=[
            pltpu.VMEM((rows + 2, 3 * mid, cols), BF16),
            pltpu.VMEM((rows, mid, cols), BF16),
            pltpu.VMEM((rows + 2, 3 * chans, cols), BF16),
            pltpu.VMEM((rows + 2, 3 * outs, cols), BF16),
            pltpu.VMEM((rows + 2, outs, cols), BF16),
            pltpu.VMEM((rows + 2, 3 * mid, cols), BF16),
            pltpu.VMEM((rows + 2, mid, cols), BF16),
            pltpu.VMEM((3 * outs, 3 * chans), F32),
            pltpu.VMEM((3 * mid, 3 * mid), F32),
            pltpu.VMEM((mid, chans), F32),
            pltpu.VMEM((mid, chans), F32),
            pltpu.VMEM((rows, 16, cols), BF16),
            pltpu.VMEM((3, mid, 3 * mid), BF16),
            pltpu.VMEM((3, mid, 3 * mid), BF16),
            pltpu.VMEM((mid, chans), BF16),
            pltpu.VMEM((3, 3, outs, chans), BF16),
            pltpu.VMEM((3, chans, 3 * outs), BF16),
            [pltpu.VMEM((depth, cols), BF16) for depth in depths],
            [pltpu.VMEM((2, depth, cols), BF16) for depth in depths],
            pltpu.SemaphoreType.DMA((16,)),
            pltpu.SemaphoreType.DMA((16,)),
        ],
        compiler_params=pltpu.CompilerParams(
            collective_id=1, has_side_effects=True, vmem_limit_bytes=56 * 1024 * 1024
        ),
        name="tile_step",
    )(
        x, anchor_labels[0], anchor_mask[0], spread, reduce_weight, spatial_weight,
        expand_weight, class_weight,
    )
    return finish(sums, mid, heads)


def finish(sums, mid, heads):
    pack, stat = sum_devices(*sums)
    chans = pack.shape[1]
    spots = layout(mid, heads)
    count = jnp.sum(stat[1])
    scale = 1.0 / count
    spatial = pack[spots[2]:spots[3], :3 * mid].reshape(3, mid, 3, mid).transpose(0, 2, 1, 3)
    return (
        jnp.sum(stat[0]) / count,
        pack[spots[0]:spots[1]] * scale,
        spatial * scale,
        pack[spots[1]:spots[2]].T * scale,
        pack[:9 * heads].reshape(3, 3, heads, chans) * scale,
    )


def solution(mesh):
    tiled = P("dp", None, "row", "col")
    return jax.shard_map(
        per_device,
        mesh=mesh,
        in_specs=(tiled, P(), P(), P(), P(), tiled, tiled),
        out_specs=(P(), P(), P(), P(), P()),
        check_vma=False,
    )
```

```python
import functools

import jax
import jax.numpy as jnp
import numpy as np
from jax import lax
from jax.experimental import pallas as pl
from jax.experimental.pallas import tpu as pltpu
from jax.sharding import PartitionSpec as P

A = 9
K = 15
GROUP = 4
WIDE = 8
LOG2E = 1.4426950408889634
LN2 = 0.6931471805599453
F32 = jnp.float32
BF16 = jnp.bfloat16
AXES = ("dp", "row", "col")


def dot(a, b):
    return jnp.dot(a, b, preferred_element_type=F32)


def dot_t(a, b):
    return lax.dot_general(a, b, (((1,), (1,)), ((), ())), preferred_element_type=F32)


def step_kernel(
    sizes, orders, heads,
    x_ref, label_ref, mask_ref, spread_ref, wr_ref, spatial_ref, we_ref, class_ref,
    loss_ref, grad_reduce_ref, grad_spatial_ref, grad_expand_ref, grad_class_ref,
    first, second, block, dlog, dzero, dsec, dsec_zero, acc_c, acc_s, acc_e, acc_r,
    code_ref, ws_ref, wsb_ref, wet_ref, wc_ref, wcb_ref, strips, got,
    stat, stat_slots, big_send, big_work, big_full, big_slots, mid_refs, tail_refs, ssem, rsem,
):
    rows, chans, cols = x_ref.shape
    mid = wr_ref.shape[0]
    outs = wc_ref.shape[2]
    me = {axis: lax.axis_index(axis) for axis in AXES}
    mesh_id = pl.DeviceIdType.MESH
    peers = lambda axis: range(1, sizes[axis])
    used = [0]

    def exists(axis, step):
        return me[axis] < sizes[axis] - 1 if step > 0 else me[axis] > 0

    barrier = pltpu.get_barrier_semaphore()
    for axis in AXES:
        for d in peers(axis):
            pl.semaphore_signal(
                barrier, inc=1, device_id={axis: lax.rem(me[axis] + d, sizes[axis])},
                device_id_type=mesh_id,
            )

    def remote(src, dst, axis, to):
        n = used[0]
        used[0] += 1
        return pltpu.make_async_remote_copy(
            src_ref=src, dst_ref=dst, send_sem=ssem.at[n], recv_sem=rsem.at[n],
            device_id={axis: to}, device_id_type=mesh_id,
        )

    def push(src, dst, axis, step):
        copy = remote(src, dst, axis, me[axis] + step)

        @pl.when(exists(axis, step))
        def _():
            copy.start()

        def finish():
            @pl.when(exists(axis, step))
            def _():
                copy.wait_send()

            @pl.when(exists(axis, -step))
            def _():
                copy.wait_recv()

        return finish

    def post(copies, src, dst, axis, d):
        copy = remote(src, dst, axis, lax.rem(me[axis] + d, sizes[axis]))
        copy.start()
        copies.append(copy)

    def settle(copies):
        for copy in copies:
            copy.wait()
        copies.clear()

    def total_of(slots):
        return sum(slots[j].astype(F32) for j in range(slots.shape[0]))

    def reduce_stats():
        copies = []
        value = stat[...]
        for k, axis in enumerate(AXES):
            slot = stat_slots[k].at[me[axis]]
            slot[...] = value
            for d in peers(axis):
                post(copies, slot, slot, axis, d)
            yield
            settle(copies)
            value = total_of(stat_slots[k])
        stat[...] = value

    def reduce_big(orders):
        share = big_send.shape[0] // len(orders)
        base = [s * share for s in range(len(orders))]
        copies = []
        part = lambda s, rows: pl.ds(pl.multiple_of(base[s], 16), rows)
        for k in range(len(AXES)):
            for s, order in enumerate(orders):
                axis, piece = order[k], big_slots[s][k].shape[1]
                for d in peers(axis):
                    to = lax.rem(me[axis] + d, sizes[axis])
                    src = big_send.at[pl.ds(pl.multiple_of(base[s] + to * piece, 16), piece)]
                    post(copies, src, big_slots[s][k].at[d - 1], axis, d)
            yield
            settle(copies)
            for s, order in enumerate(orders):
                axis, piece = order[k], big_slots[s][k].shape[1]
                base[s] = base[s] + me[axis] * piece
                at = part(s, piece)
                value = (big_work if k else big_send)[at, :].astype(F32)
                for d in peers(axis):
                    value = value + big_slots[s][k][d - 1].astype(F32)
                if k < len(AXES) - 1:
                    big_work[at, :] = value
                    big_send[at, :] = value.astype(BF16)
                else:
                    big_full[at, :] = value.astype(BF16)
        for k in reversed(range(len(AXES))):
            for s, order in enumerate(orders):
                axis, piece = order[k], big_slots[s][k].shape[1]
                at = part(s, piece)
                for d in peers(axis):
                    post(copies, big_full.at[at], big_full.at[at], axis, d)
                base[s] = base[s] - me[axis] * piece
            yield
            settle(copies)

    def reduce_small(refs):
        send, full, across, tile_slots, row_slots = refs
        piece = across.shape[1]
        copies = []
        mine = pl.ds(pl.multiple_of(me["col"] * piece, 16), piece)
        across[me["col"]] = send[mine, :]
        for d in peers("col"):
            to = lax.rem(me["col"] + d, sizes["col"])
            src = send.at[pl.ds(pl.multiple_of(to * piece, 16), piece)]
            post(copies, src, across.at[me["col"]], "col", d)
        yield
        settle(copies)
        value = total_of(across)
        for axis, slots in (("dp", tile_slots), ("row", row_slots)):
            slot = slots.at[me[axis]]
            slot[...] = value.astype(slots.dtype)
            for d in peers(axis):
                post(copies, slot, slot, axis, d)
            yield
            settle(copies)
            value = total_of(slots)
        full[mine, :] = value.astype(full.dtype)
        for d in peers("col"):
            post(copies, full.at[mine], full.at[mine], "col", d)
        yield
        settle(copies)

    def loop(steps, body, init=0):
        return lax.fori_loop(0, steps, body, init)

    def cat(ref, at, count, low=None, high=None):
        part = slice(low, high)
        return jnp.concatenate([ref[at + k, part, :] for k in range(count)], axis=1)

    def spread_rows(ref, at, value, low=None, high=None):
        for k in range(value.shape[1] // cols):
            ref[at + k, low:high, :] = value[:, k * cols:(k + 1) * cols]

    def clear_edges(n, field, depth):
        blank = jnp.zeros((depth, cols), BF16)

        @pl.when(jnp.logical_not(exists("row", -1)))
        def _():
            field[0, depth:2 * depth, :] = blank

        @pl.when(jnp.logical_not(exists("row", 1)))
        def _():
            field[rows + 1, depth:2 * depth, :] = blank

        for side in range(2):
            @pl.when(jnp.logical_not(exists("col", 1 if side else -1)))
            def _():
                got[n][side] = blank

    def send_rows(n, field, depth):
        down = push(
            field.at[rows, pl.ds(depth, depth)], field.at[0, pl.ds(depth, depth)], "row", 1
        )
        up = push(
            field.at[1, pl.ds(depth, depth)],
            field.at[rows + 1, pl.ds(depth, depth)], "row", -1,
        )
        return down, up

    def publish(n, field, depth, at, value):
        lane = lax.broadcasted_iota(jnp.int32, (depth, cols), 1) // 2
        for k in range(value.shape[1] // cols):
            row = value[:, k * cols:(k + 1) * cols]
            i = at + k
            field[i, depth:2 * depth, :] = row
            field[i, :depth, :] = pltpu.roll(row, 1, 1)
            field[i, 2 * depth:, :] = pltpu.roll(row, cols - 1, 1)
            strips[n][...] = jnp.where(lane == i, pltpu.roll(row, 2 * i + 1, 1), strips[n][...])

    def send_strip(n, field, depth, held):
        for wait in held:
            wait()
        for i in (0, rows + 1):
            publish(n, field, depth, i, field[i, depth:2 * depth, :])
        right = push(strips[n], got[n].at[0], "col", 1)
        left = push(strips[n], got[n].at[1], "col", -1)
        return right, left

    def widen(n, field, depth, held):
        for wait in held:
            wait()
        lane = lax.broadcasted_iota(jnp.int32, (depth, cols), 1)
        before, after = got[n][0], got[n][1]
        for i in range(rows + 2):
            field[i, :depth, :] = jnp.where(
                lane == 0, pltpu.roll(before, (cols - 2 * i) % cols, 1), field[i, :depth, :]
            )
            field[i, 2 * depth:, :] = jnp.where(
                lane == cols - 1, pltpu.roll(after, (cols - 2 - 2 * i) % cols, 1),
                field[i, 2 * depth:, :],
            )

    def conv(weight, field, at):
        return sum(dot(weight(dy), cat(field, at + dy, GROUP)) for dy in range(3))

    def sweep(body, between, init=0, halfway=None):
        groups = rows // GROUP
        carry = loop(2, lambda j, c: body(j * (groups - 1), c), init)
        held = between()
        half = groups // 2 - 1
        carry = loop(half, lambda j, c: body(j + 1, c), carry)
        if halfway is not None:
            halfway()
        return held, loop(groups - 2 - half, lambda j, c: body(j + 1 + half, c), carry)

    fields = [(first, mid), (block, chans), (dlog, outs), (dsec, mid)]
    for n, (field, depth) in enumerate(fields):
        clear_edges(n, field, depth)
        strips[n][...] = jnp.zeros((depth, cols), BF16)
    for ref in (dzero, dsec_zero):
        ref[0] = jnp.zeros(ref.shape[1:], BF16)
        ref[rows + 1] = jnp.zeros(ref.shape[1:], BF16)
    for ref in (acc_c, acc_s, acc_e, acc_r):
        ref[...] = jnp.zeros_like(ref)
    big_send[...] = jnp.zeros_like(big_send)
    pl.semaphore_wait(barrier, sum(sizes[axis] - 1 for axis in AXES))

    def make_first(i, c):
        z = dot(wr_ref[...], cat(x_ref, i * GROUP, GROUP))
        publish(0, first, mid, i * GROUP + 1, jnp.maximum(z, 0.0).astype(BF16))
        return c

    held, _ = sweep(make_first, lambda: send_rows(0, first, mid))
    for dy in range(3):
        for dx in range(3):
            ws_ref[dy, :, dx * mid:(dx + 1) * mid] = spatial_ref[dy, dx]
            wc_ref[dy, dx, :heads, :] = class_ref[dy, dx]
            wc_ref[dy, dx, heads:, :] = jnp.zeros((outs - heads, chans), BF16)
    for h in range(rows):
        code = jnp.where(mask_ref[:, h, :] > 0, label_ref[:, h, :], 64)
        code_ref[h, :A, :] = code.astype(F32).astype(BF16)
        code_ref[h, A:, :] = jnp.ones((16 - A, cols), BF16)
    held = send_strip(0, first, mid, held)

    def turned(parts):
        size = parts[0].shape[1]
        eye = jnp.where(
            lax.broadcasted_iota(jnp.int32, (size, size), 0)
            == lax.broadcasted_iota(jnp.int32, (size, size), 1), 1.0, 0.0,
        ).astype(BF16)
        return dot_t(eye, jnp.concatenate(parts, axis=0)).astype(BF16)

    wet_ref[...] = turned([we_ref[...]])
    for dy in range(3):
        wsb_ref[dy] = turned([spatial_ref[2 - dy, 2 - dx] for dx in range(3)])
        wcb_ref[dy] = turned([wc_ref[2 - dy, 2 - dx] for dx in range(3)])
    widen(0, first, mid, held)

    def make_block(i, c):
        s = jnp.maximum(conv(lambda dy: ws_ref[dy], first, i * GROUP), 0.0).astype(BF16)
        spread_rows(second, i * GROUP, s)
        b = jnp.maximum(cat(x_ref, i * GROUP, GROUP).astype(F32) + dot(we_ref[...], s), 0.0)
        publish(1, block, chans, i * GROUP + 1, b.astype(BF16))
        return c

    held, _ = sweep(make_block, lambda: send_rows(1, block, chans))
    held = send_strip(1, block, chans, held)
    widen(1, block, chans, held)

    def class_rows(dy):
        return jnp.concatenate([wc_ref[dy, dx] for dx in range(3)], axis=1)

    def make_dlog(i, carry):
        total, count = carry
        z = conv(class_rows, block, i * GROUP)
        code = cat(code_ref, i * GROUP, GROUP)
        gap = dot(spread_ref[...], code)
        target = gap == 0.0
        alpha = jnp.where(target, 0.25, jnp.where(gap > 32.0, 0.0, 0.75))
        z = z * LOG2E
        u = jnp.where(target, -z, z)
        e = jnp.exp2(-jnp.abs(u))
        soft = jnp.maximum(u, 0.0) + jnp.log2(1.0 + e)
        prob = jnp.exp2(u - soft)
        scaled = alpha * prob * prob
        total = total + jnp.sum(scaled * soft, axis=0, keepdims=True)
        slope = scaled * ((2.0 * LN2 - 2.0 * LN2 * prob) * soft + prob)
        d = jnp.where(target, -slope, slope).astype(BF16)
        publish(2, dlog, outs, i * GROUP + 1, d)
        spread_rows(dzero, i * GROUP + 1, d)
        codes = code.astype(F32)
        row = lax.broadcasted_iota(jnp.int32, codes.shape, 0)
        hit = jnp.where((codes > 0.5) & (codes < 32.0) & (row < A), 1.0, 0.0)
        count = count + jnp.sum(hit, axis=0, keepdims=True)
        return total, count

    zero = jnp.zeros((1, GROUP * cols), F32)
    held, (total, count) = sweep(make_dlog, lambda: send_rows(2, dlog, outs), (zero, zero))
    fold = lambda v: sum(v[:, k * 128:(k + 1) * 128] for k in range(v.shape[1] // 128))
    stat[0:1, :] = fold(total) * LN2
    stat[1:2, :] = fold(count)
    stat[2:, :] = jnp.zeros((6, 128), F32)
    stats = reduce_stats()
    next(stats)

    def weight_sum(acc, grad, field):
        depth = grad.shape[1]

        def add(i, c):
            at = i * WIDE + 1
            tall = jnp.concatenate([cat(grad, at + 1 - dy, WIDE) for dy in range(3)], axis=0)
            acc[...] += dot_t(tall, cat(field, at, WIDE))
            return c

        loop(rows // WIDE, add)
        acc[:depth, :] += dot_t(grad[1], field[0])
        acc[2 * depth:, :] += dot_t(grad[rows], field[rows + 1])

    def advance(*steps):
        for step in steps:
            next(step, None)

    weight_sum(acc_c, dzero, block)
    share = big_send.shape[0] // 3
    for dy in range(3):
        for dx in range(3):
            at = dy * share + dx * outs
            big_send[at:at + outs, :] = acc_c[
                dy * outs:(dy + 1) * outs, dx * chans:(dx + 1) * chans
            ].astype(BF16)
    big = reduce_big(orders)
    advance(big, stats)
    held = send_strip(2, dlog, outs, held)
    widen(2, dlog, outs, held)

    def make_dsec(i, c):
        g = conv(lambda dy: wcb_ref[dy], dlog, i * GROUP)
        b = cat(block, i * GROUP + 1, GROUP, chans, 2 * chans).astype(F32)
        ds = jnp.where(b > 0.0, g, 0.0).astype(BF16)
        s = cat(second, i * GROUP, GROUP)
        acc_e[...] += dot_t(s, ds)
        h = dot(wet_ref[...], ds)
        d = jnp.where(s.astype(F32) > 0.0, h, 0.0).astype(BF16)
        publish(3, dsec, mid, i * GROUP + 1, d)
        spread_rows(dsec_zero, i * GROUP + 1, d)
        return c

    def after_edges():
        sent = send_rows(3, dsec, mid)
        advance(big, stats)
        return sent

    held, _ = sweep(make_dsec, after_edges, halfway=lambda: advance(big, stats))
    advance(big)
    weight_sum(acc_s, dsec_zero, first)
    held = send_strip(3, dsec, mid, held)
    mid_send, mid_full = mid_refs[:2]
    mid_send[:mid, :] = acc_e[...].astype(mid_send.dtype)
    mid_send[mid:, :] = jnp.zeros((mid_send.shape[0] - mid, chans), mid_send.dtype)
    mid_send[mid:4 * mid, :3 * mid] = acc_s[...].astype(mid_send.dtype)
    middle = reduce_small(mid_refs)
    advance(middle)
    widen(3, dsec, mid, held)
    advance(big, middle)

    def make_dfirst(i, c):
        g = conv(lambda dy: wsb_ref[dy], dsec, i * GROUP)
        f = cat(first, i * GROUP + 1, GROUP, mid, 2 * mid).astype(F32)
        df = jnp.where(f > 0.0, g, 0.0).astype(BF16)
        acc_r[...] += dot_t(df, cat(x_ref, i * GROUP, GROUP))
        return c

    loop(rows // GROUP, make_dfirst)
    tail_send, tail_full = tail_refs[:2]
    tail_send[:mid, :] = acc_r[...].astype(tail_send.dtype)
    if tail_send.shape[0] > mid:
        tail_send[mid:, :] = jnp.zeros((tail_send.shape[0] - mid, chans), tail_send.dtype)
    tail = reduce_small(tail_refs)
    advance(tail, big, middle)
    scale = 1.0 / jnp.sum(stat[1:2, :], axis=1, keepdims=True)
    loss_ref[...] = jnp.sum(stat[0:1, :], axis=1, keepdims=True) * scale
    advance(tail, middle)
    advance(big)
    for dy in range(3):
        for dx in range(3):
            at = dy * share + dx * outs
            grad_class_ref[dy, dx] = big_full[at:at + outs, :].astype(F32)[:heads] * scale
    advance(tail, middle)
    grad_expand_ref[...] = (mid_full[:mid, :].astype(F32) * scale).T
    for dy in range(3):
        part = mid_full[(dy + 1) * mid:(dy + 2) * mid, :].astype(F32) * scale
        for dx in range(3):
            grad_spatial_ref[dy, dx] = part[:, dx * mid:(dx + 1) * mid]
    advance(tail)
    advance(tail)
    grad_reduce_ref[...] = tail_full[:mid, :].astype(F32) * scale


def per_device(
    inputs, reduce_weight, spatial_weight, expand_weight, class_weight, anchor_labels, anchor_mask
):
    tiles, chans, rows, cols = inputs.shape
    assert tiles == 1
    mid = reduce_weight.shape[0]
    heads = class_weight.shape[2]
    outs = -(-heads // 16) * 16
    sizes = {axis: lax.axis_size(axis) for axis in AXES}

    x = inputs[0].transpose(1, 0, 2)

    spread = np.zeros((outs, 16), np.float32)
    spread[np.arange(heads), np.arange(heads) // K] = 1.0
    spread[np.arange(heads), A] = -1.0 - np.arange(heads) % K
    spread[heads:, A] = 64.0
    spread = jnp.asarray(spread, BF16)

    depths = (mid, chans, outs, mid)
    orders = [AXES[s:] + AXES[:s] for s in range(len(AXES))]
    devices = int(np.prod([sizes[axis] for axis in AXES]))
    share = -(-3 * outs // (16 * devices)) * 16 * devices

    def slots(order):
        size, out = share, []
        for axis in order:
            size //= sizes[axis]
            out.append(pltpu.VMEM((max(sizes[axis] - 1, 1), size, chans), BF16))
        return out

    def small(need, kind):
        piece = -(-need // (16 * sizes["col"])) * 16
        full = pltpu.VMEM((piece * sizes["col"], chans), kind)
        return [full, full] + [
            pltpu.VMEM((sizes[axis], piece, chans), kind) for axis in ("col", "dp", "row")
        ]

    copies = 16 + sum(
        (sizes[axis] - 1) * (1 + 2 * len(orders) + 2 * (2 if axis == "col" else 1))
        for axis in AXES
    )
    outputs = [(1, 1), (mid, chans), (3, 3, mid, mid), (chans, mid), class_weight.shape]

    loss, *grads = pl.pallas_call(
        functools.partial(step_kernel, sizes, orders, heads),
        out_shape=[jax.ShapeDtypeStruct(shape, F32) for shape in outputs],
        in_specs=[pl.BlockSpec(memory_space=pltpu.VMEM)] * 8,
        out_specs=[pl.BlockSpec(memory_space=pltpu.VMEM)] * 5,
        scratch_shapes=[
            pltpu.VMEM((rows + 2, 3 * mid, cols), BF16),
            pltpu.VMEM((rows, mid, cols), BF16),
            pltpu.VMEM((rows + 2, 3 * chans, cols), BF16),
            pltpu.VMEM((rows + 2, 3 * outs, cols), BF16),
            pltpu.VMEM((rows + 2, outs, cols), BF16),
            pltpu.VMEM((rows + 2, 3 * mid, cols), BF16),
            pltpu.VMEM((rows + 2, mid, cols), BF16),
            pltpu.VMEM((3 * outs, 3 * chans), F32),
            pltpu.VMEM((3 * mid, 3 * mid), F32),
            pltpu.VMEM((mid, chans), F32),
            pltpu.VMEM((mid, chans), F32),
            pltpu.VMEM((rows, 16, cols), BF16),
            pltpu.VMEM((3, mid, 3 * mid), BF16),
            pltpu.VMEM((3, mid, 3 * mid), BF16),
            pltpu.VMEM((mid, chans), BF16),
            pltpu.VMEM((3, 3, outs, chans), BF16),
            pltpu.VMEM((3, chans, 3 * outs), BF16),
            [pltpu.VMEM((depth, cols), BF16) for depth in depths],
            [pltpu.VMEM((2, depth, cols), BF16) for depth in depths],
            pltpu.VMEM((8, 128), F32),
            [pltpu.VMEM((sizes[axis], 8, 128), F32) for axis in AXES],
            pltpu.VMEM((3 * share, chans), BF16),
            pltpu.VMEM((3 * share, chans), F32),
            pltpu.VMEM((3 * share, chans), BF16),
            [slots(order) for order in orders],
            small(4 * mid, BF16),
            small(mid, F32),
            pltpu.SemaphoreType.DMA((copies,)),
            pltpu.SemaphoreType.DMA((copies,)),
        ],
        compiler_params=pltpu.CompilerParams(
            collective_id=1, has_side_effects=True, vmem_limit_bytes=60 * 1024 * 1024
        ),
        name="tile_step",
    )(
        x, anchor_labels[0], anchor_mask[0], spread, reduce_weight, spatial_weight,
        expand_weight, class_weight,
    )
    return loss.reshape(()), *grads


def solution(mesh):
    tiled = P("dp", None, "row", "col")
    return jax.shard_map(
        per_device,
        mesh=mesh,
        in_specs=(tiled, P(), P(), P(), P(), tiled, tiled),
        out_specs=(P(), P(), P(), P(), P()),
        check_vma=False,
    )
```

```python
import functools

import jax
import jax.numpy as jnp
import numpy as np
from jax import lax
from jax.experimental import pallas as pl
from jax.experimental.pallas import tpu as pltpu
from jax.sharding import PartitionSpec as P

A = 9
K = 15
GROUP = 4
WIDE = 8
LOG2E = 1.4426950408889634
LN2 = 0.6931471805599453
F32 = jnp.float32
BF16 = jnp.bfloat16
AXES = ("dp", "row", "col")


def dot(a, b):
    return jnp.dot(a, b, preferred_element_type=F32)


def dot_t(a, b):
    return lax.dot_general(a, b, (((1,), (1,)), ((), ())), preferred_element_type=F32)


def step_kernel(
    sizes, heads,
    x_ref, label_ref, mask_ref, spread_ref, wr_ref, spatial_ref, wet_ref, class_ref,
    loss_ref, scale_ref, small_out, spatial_out, class_out,
    first, second, block, dlog, dzero, dsec, dsec_zero, acc_c, acc_s, acc_e, acc_r,
    code_ref, ws_ref, wsb_ref, we_ref, wc_ref, wcb_ref, strips, got,
    stat, stat_slots, big_refs, mid_refs, tail_refs, ssem, rsem, osem,
):
    rows, chans, cols = x_ref.shape
    mid = wr_ref.shape[0]
    outs = wc_ref.shape[2]
    me = {axis: lax.axis_index(axis) for axis in AXES}
    mesh_id = pl.DeviceIdType.MESH
    peers = lambda axis: range(1, sizes[axis])
    used = [0]

    def exists(axis, step):
        return me[axis] < sizes[axis] - 1 if step > 0 else me[axis] > 0

    plane = [
        (d, e) for d in range(sizes["dp"]) for e in range(sizes["col"]) if d or e
    ]
    shift = lambda axis, d: lax.rem(me[axis] + d, sizes[axis])
    across = [{"dp": shift("dp", d), "col": shift("col", e)} for d, e in plane]
    along = [{"row": shift("row", d)} for d in peers("row")]
    place = lambda to: to["dp"] * sizes["col"] + to["col"]

    barrier = pltpu.get_barrier_semaphore()
    for to in across + along:
        pl.semaphore_signal(barrier, inc=1, device_id=to, device_id_type=mesh_id)

    def remote(src, dst, to):
        n = used[0]
        used[0] += 1
        return pltpu.make_async_remote_copy(
            src_ref=src, dst_ref=dst, send_sem=ssem.at[n], recv_sem=rsem.at[n],
            device_id=to, device_id_type=mesh_id,
        )

    def push(src, dst, axis, step):
        copy = remote(src, dst, {axis: me[axis] + step})

        @pl.when(exists(axis, step))
        def _():
            copy.start()

        def finish():
            @pl.when(exists(axis, step))
            def _():
                copy.wait_send()

            @pl.when(exists(axis, -step))
            def _():
                copy.wait_recv()

        return finish

    def settle(copies):
        for copy in copies:
            copy.wait()

    def total_of(slots):
        return sum(slots[j].astype(F32) for j in range(slots.shape[0]))

    def share_all(slots, value, targets, mine):
        slot = slots.at[mine]
        slot[...] = value.astype(slots.dtype)
        copies = [remote(slot, slot, to) for to in targets]
        for copy in copies:
            copy.start()
        return copies

    def reduce_whole(value, plane_slots, row_slots, store):
        copies = share_all(plane_slots, value, across, place(me))
        yield
        settle(copies)
        copies = share_all(row_slots, total_of(plane_slots), along, me["row"])
        yield
        settle(copies)
        store(total_of(row_slots))

    def reduce_split(refs):
        send, full, plane_slots, row_slots = refs
        piece = row_slots.shape[1]
        part = lambda to: pl.ds(pl.multiple_of(place(to) * piece, 16), piece)
        slot = plane_slots.at[place(me)]
        slot[...] = send[part(me), :]
        copies = [remote(send.at[part(to)], slot, to) for to in across]
        for copy in copies:
            copy.start()
        yield
        settle(copies)
        copies = share_all(row_slots, total_of(plane_slots), along, me["row"])
        yield
        settle(copies)
        full[part(me), :] = total_of(row_slots).astype(full.dtype)
        copies = [remote(full.at[part(me)], full.at[part(me)], to) for to in across]
        for copy in copies:
            copy.start()
        yield
        settle(copies)

    def advance(*steps):
        for step in steps:
            next(step, None)

    def loop(steps, body, init=0):
        return lax.fori_loop(0, steps, body, init)

    def cat(ref, at, count, low=None, high=None):
        part = slice(low, high)
        return jnp.concatenate([ref[at + k, part, :] for k in range(count)], axis=1)

    def spread_rows(ref, at, value, low=None, high=None):
        for k in range(value.shape[1] // cols):
            ref[at + k, low:high, :] = value[:, k * cols:(k + 1) * cols]

    def clear_edges(n, field, depth):
        blank = jnp.zeros((depth, cols), BF16)

        @pl.when(jnp.logical_not(exists("row", -1)))
        def _():
            field[0, depth:2 * depth, :] = blank

        @pl.when(jnp.logical_not(exists("row", 1)))
        def _():
            field[rows + 1, depth:2 * depth, :] = blank

        for side in range(2):
            @pl.when(jnp.logical_not(exists("col", 1 if side else -1)))
            def _():
                got[n][side] = blank

    def send_rows(n, field, depth):
        down = push(
            field.at[rows, pl.ds(depth, depth)], field.at[0, pl.ds(depth, depth)], "row", 1
        )
        up = push(
            field.at[1, pl.ds(depth, depth)],
            field.at[rows + 1, pl.ds(depth, depth)], "row", -1,
        )
        return down, up

    def publish(n, field, depth, at, value):
        lane = lax.broadcasted_iota(jnp.int32, (depth, cols), 1) // 2
        for k in range(value.shape[1] // cols):
            row = value[:, k * cols:(k + 1) * cols]
            i = at + k
            field[i, depth:2 * depth, :] = row
            field[i, :depth, :] = pltpu.roll(row, 1, 1)
            field[i, 2 * depth:, :] = pltpu.roll(row, cols - 1, 1)
            strips[n][...] = jnp.where(lane == i, pltpu.roll(row, 2 * i + 1, 1), strips[n][...])

    def send_strip(n, field, depth, held):
        for wait in held:
            wait()
        for i in (0, rows + 1):
            publish(n, field, depth, i, field[i, depth:2 * depth, :])
        right = push(strips[n], got[n].at[0], "col", 1)
        left = push(strips[n], got[n].at[1], "col", -1)
        return right, left

    def widen(n, field, depth, held):
        for wait in held:
            wait()
        lane = lax.broadcasted_iota(jnp.int32, (depth, cols), 1)
        before, after = got[n][0], got[n][1]
        for i in range(rows + 2):
            field[i, :depth, :] = jnp.where(
                lane == 0, pltpu.roll(before, (cols - 2 * i) % cols, 1), field[i, :depth, :]
            )
            field[i, 2 * depth:, :] = jnp.where(
                lane == cols - 1, pltpu.roll(after, (cols - 2 - 2 * i) % cols, 1),
                field[i, 2 * depth:, :],
            )

    def conv(weight, field, at):
        return sum(dot(weight(dy), cat(field, at + dy, GROUP)) for dy in range(3))

    def sweep(body, between, init=0, halfway=None):
        groups = rows // GROUP
        carry = loop(2, lambda j, c: body(j * (groups - 1), c), init)
        held = between()
        half = groups // 2 - 1
        carry = loop(half, lambda j, c: body(j + 1, c), carry)
        if halfway is not None:
            halfway()
        return held, loop(groups - 2 - half, lambda j, c: body(j + 1 + half, c), carry)

    fields = [(first, mid), (block, chans), (dlog, outs), (dsec, mid)]
    for n, (field, depth) in enumerate(fields):
        clear_edges(n, field, depth)
        strips[n][...] = jnp.zeros((depth, cols), BF16)
    for ref in (dzero, dsec_zero):
        ref[0] = jnp.zeros(ref.shape[1:], BF16)
        ref[rows + 1] = jnp.zeros(ref.shape[1:], BF16)
    for ref in (acc_e, acc_r, mid_refs[0]) + tuple(refs[0] for refs in big_refs):
        ref[...] = jnp.zeros_like(ref)
    pl.semaphore_wait(barrier, len(across) + len(along))

    def make_first(i, c):
        z = dot(wr_ref[...], cat(x_ref, i * GROUP, GROUP))
        publish(0, first, mid, i * GROUP + 1, jnp.maximum(z, 0.0).astype(BF16))
        return c

    held, _ = sweep(make_first, lambda: send_rows(0, first, mid))
    for dy in range(3):
        for dx in range(3):
            ws_ref[dy, :, dx * mid:(dx + 1) * mid] = spatial_ref[dy, dx]
            wc_ref[dy, dx, :heads, :] = class_ref[dy, dx]
            wc_ref[dy, dx, heads:, :] = jnp.zeros((outs - heads, chans), BF16)
    for h in range(rows):
        code = jnp.where(mask_ref[:, h, :] > 0, label_ref[:, h, :], 64)
        code_ref[h, :A, :] = code.astype(F32).astype(BF16)
        code_ref[h, A:, :] = jnp.ones((16 - A, cols), BF16)
    held = send_strip(0, first, mid, held)

    def turned(parts):
        size = parts[0].shape[1]
        eye = jnp.where(
            lax.broadcasted_iota(jnp.int32, (size, size), 0)
            == lax.broadcasted_iota(jnp.int32, (size, size), 1), 1.0, 0.0,
        ).astype(BF16)
        return dot_t(eye, jnp.concatenate(parts, axis=0)).astype(BF16)

    we_ref[...] = turned([wet_ref[...]])
    for dy in range(3):
        wsb_ref[dy] = turned([spatial_ref[2 - dy, 2 - dx] for dx in range(3)])
        wcb_ref[dy] = turned([wc_ref[2 - dy, 2 - dx] for dx in range(3)])
    widen(0, first, mid, held)

    def make_block(i, c):
        s = jnp.maximum(conv(lambda dy: ws_ref[dy], first, i * GROUP), 0.0).astype(BF16)
        spread_rows(second, i * GROUP, s)
        b = jnp.maximum(cat(x_ref, i * GROUP, GROUP).astype(F32) + dot(we_ref[...], s), 0.0)
        publish(1, block, chans, i * GROUP + 1, b.astype(BF16))
        return c

    held, _ = sweep(make_block, lambda: send_rows(1, block, chans))
    held = send_strip(1, block, chans, held)
    widen(1, block, chans, held)

    def class_rows(dy):
        return jnp.concatenate([wc_ref[dy, dx] for dx in range(3)], axis=1)

    def make_dlog(i, carry):
        total, count = carry
        z = conv(class_rows, block, i * GROUP)
        code = cat(code_ref, i * GROUP, GROUP)
        gap = dot(spread_ref[...], code)
        target = gap == 0.0
        alpha = jnp.where(target, 0.25, jnp.where(gap > 32.0, 0.0, 0.75))
        z = z * LOG2E
        u = jnp.where(target, -z, z)
        e = jnp.exp2(-jnp.abs(u))
        soft = jnp.maximum(u, 0.0) + jnp.log2(1.0 + e)
        prob = jnp.exp2(u - soft)
        scaled = alpha * prob * prob
        total = total + jnp.sum(scaled * soft, axis=0, keepdims=True)
        slope = scaled * ((2.0 * LN2 - 2.0 * LN2 * prob) * soft + prob)
        d = jnp.where(target, -slope, slope).astype(BF16)
        publish(2, dlog, outs, i * GROUP + 1, d)
        spread_rows(dzero, i * GROUP + 1, d)
        codes = code.astype(F32)
        row = lax.broadcasted_iota(jnp.int32, codes.shape, 0)
        hit = jnp.where((codes > 0.5) & (codes < 32.0) & (row < A), 1.0, 0.0)
        count = count + jnp.sum(hit, axis=0, keepdims=True)
        return total, count

    zero = jnp.zeros((1, GROUP * cols), F32)
    held, (total, count) = sweep(make_dlog, lambda: send_rows(2, dlog, outs), (zero, zero))
    fold = lambda v: sum(v[:, k * 128:(k + 1) * 128] for k in range(v.shape[1] // 128))
    stat[0:1, :] = fold(total) * LN2
    stat[1:2, :] = fold(count)
    stat[2:, :] = jnp.zeros((6, 128), F32)

    def keep(value):
        stat[...] = value

    stats = reduce_whole(stat[...], *stat_slots, keep)
    advance(stats)
    held = send_strip(2, dlog, outs, held)

    def weight_sum(acc, grad, field, low, high):
        depth = grad.shape[1]
        acc[...] = jnp.zeros_like(acc)

        def add(i, c):
            at = i * WIDE + 1
            tall = jnp.concatenate([cat(grad, at + 1 - dy, WIDE) for dy in range(3)], axis=0)
            acc[...] += dot_t(tall, cat(field, at, WIDE, low, high))
            return c

        loop(rows // WIDE, add)
        acc[:depth, :] += dot_t(grad[1], field[0, low:high])
        acc[2 * depth:, :] += dot_t(grad[rows], field[rows + 1, low:high])

    bigs = []
    for dx in range(3):
        low, high = dx * chans, (dx + 1) * chans
        weight_sum(acc_c, dzero, block, low, high)
        send = big_refs[dx][0]
        send[:3 * outs, :] = acc_c[...].astype(BF16)
        bigs.append(reduce_split(big_refs[dx]))
        advance(bigs[dx])
    widen(2, dlog, outs, held)

    def make_dsec(i, c):
        g = conv(lambda dy: wcb_ref[dy], dlog, i * GROUP)
        b = cat(block, i * GROUP + 1, GROUP, chans, 2 * chans).astype(F32)
        ds = jnp.where(b > 0.0, g, 0.0).astype(BF16)
        s = cat(second, i * GROUP, GROUP)
        acc_e[...] += dot_t(s, ds)
        h = dot(wet_ref[...], ds)
        d = jnp.where(s.astype(F32) > 0.0, h, 0.0).astype(BF16)
        publish(3, dsec, mid, i * GROUP + 1, d)
        spread_rows(dsec_zero, i * GROUP + 1, d)
        return c

    def after_edges():
        sent = send_rows(3, dsec, mid)
        advance(bigs[0], stats)
        return sent

    held, _ = sweep(make_dsec, after_edges, halfway=lambda: advance(*bigs[1:]))
    held = send_strip(3, dsec, mid, held)
    advance(bigs[0], stats)
    weight_sum(acc_s, dsec_zero, first, 0, 3 * mid)
    mid_send, mid_full = mid_refs[:2]
    mid_send[:mid, :] = acc_e[...].astype(BF16)
    mid_send[mid:4 * mid, :3 * mid] = acc_s[...].astype(BF16)
    middle = reduce_split(mid_refs)
    advance(middle)
    advance(bigs[1])
    widen(3, dsec, mid, held)
    advance(bigs[2])

    def make_dfirst(i, c):
        g = conv(lambda dy: wsb_ref[dy], dsec, i * GROUP)
        f = cat(first, i * GROUP + 1, GROUP, mid, 2 * mid).astype(F32)
        df = jnp.where(f > 0.0, g, 0.0).astype(BF16)
        acc_r[...] += dot_t(df, cat(x_ref, i * GROUP, GROUP))
        return c

    loop(rows // GROUP, make_dfirst)

    def place_tail(value):
        small_out[:mid, :] = value

    tail = reduce_whole(acc_r[...], *tail_refs, place_tail)
    advance(tail, middle, *bigs)
    outgoing = []
    for dx in range(3):
        for dy in range(3):
            outgoing.append(pltpu.make_async_copy(
                big_refs[dx][1].at[pl.ds(dy * outs, outs)], class_out.at[dy, dx],
                osem.at[3 * dx + dy],
            ))
            outgoing[-1].start()
    scale = 1.0 / jnp.sum(stat[1:2, :], axis=1, keepdims=True)
    scale_ref[...] = scale
    loss_ref[...] = jnp.sum(stat[0:1, :], axis=1, keepdims=True) * scale
    advance(tail, middle)
    advance(middle)
    small_out[mid:, :] = mid_full[:mid, :].astype(F32)
    for dy in range(3):
        part = mid_full[(dy + 1) * mid:(dy + 2) * mid, :].astype(F32)
        for dx in range(3):
            spatial_out[dy, dx] = part[:, dx * mid:(dx + 1) * mid]
    advance(tail)
    for copy in outgoing:
        copy.wait()


def per_device(
    inputs, reduce_weight, spatial_weight, expand_weight, class_weight, anchor_labels, anchor_mask
):
    tiles, chans, rows, cols = inputs.shape
    assert tiles == 1
    mid = reduce_weight.shape[0]
    heads = class_weight.shape[2]
    outs = -(-heads // 16) * 16
    sizes = {axis: lax.axis_size(axis) for axis in AXES}

    x = inputs[0].transpose(1, 0, 2)

    spread = np.zeros((outs, 16), np.float32)
    spread[np.arange(heads), np.arange(heads) // K] = 1.0
    spread[np.arange(heads), A] = -1.0 - np.arange(heads) % K
    spread[heads:, A] = 64.0
    spread = jnp.asarray(spread, BF16)

    depths = (mid, chans, outs, mid)
    across = sizes["dp"] * sizes["col"]

    def split_refs(need):
        piece = -(-need // (16 * across)) * 16
        full = pltpu.VMEM((piece * across, chans), BF16)
        return [full, full] + [
            pltpu.VMEM((count, piece, chans), BF16) for count in (across, sizes["row"])
        ]

    def whole_refs(shape, kind):
        return [pltpu.VMEM((count,) + shape, kind) for count in (across, sizes["row"])]

    copies = 16 + 6 * (across - 1) + 4 * (across - 1) + 6 * (sizes["row"] - 1)
    outputs = [
        ((1, 1), F32), ((1, 1), F32), ((2 * mid, chans), F32), ((3, 3, mid, mid), F32),
        ((3, 3, outs, chans), BF16),
    ]

    loss, scale, small, spatial, wide = pl.pallas_call(
        functools.partial(step_kernel, sizes, heads),
        out_shape=[jax.ShapeDtypeStruct(*output) for output in outputs],
        in_specs=[pl.BlockSpec(memory_space=pltpu.VMEM)] * 8,
        out_specs=[pl.BlockSpec(memory_space=pltpu.VMEM)] * 4
        + [pl.BlockSpec(memory_space=pl.ANY)],
        scratch_shapes=[
            pltpu.VMEM((rows + 2, 3 * mid, cols), BF16),
            pltpu.VMEM((rows, mid, cols), BF16),
            pltpu.VMEM((rows + 2, 3 * chans, cols), BF16),
            pltpu.VMEM((rows + 2, 3 * outs, cols), BF16),
            pltpu.VMEM((rows + 2, outs, cols), BF16),
            pltpu.VMEM((rows + 2, 3 * mid, cols), BF16),
            pltpu.VMEM((rows + 2, mid, cols), BF16),
            pltpu.VMEM((3 * outs, chans), F32),
            pltpu.VMEM((3 * mid, 3 * mid), F32),
            pltpu.VMEM((mid, chans), F32),
            pltpu.VMEM((mid, chans), F32),
            pltpu.VMEM((rows, 16, cols), BF16),
            pltpu.VMEM((3, mid, 3 * mid), BF16),
            pltpu.VMEM((3, mid, 3 * mid), BF16),
            pltpu.VMEM((chans, mid), BF16),
            pltpu.VMEM((3, 3, outs, chans), BF16),
            pltpu.VMEM((3, chans, 3 * outs), BF16),
            [pltpu.VMEM((depth, cols), BF16) for depth in depths],
            [pltpu.VMEM((2, depth, cols), BF16) for depth in depths],
            pltpu.VMEM((8, 128), F32),
            whole_refs((8, 128), F32),
            [split_refs(3 * outs) for _ in range(3)],
            split_refs(4 * mid),
            whole_refs((mid, chans), BF16),
            pltpu.SemaphoreType.DMA((copies,)),
            pltpu.SemaphoreType.DMA((copies,)),
            pltpu.SemaphoreType.DMA((9,)),
        ],
        compiler_params=pltpu.CompilerParams(
            collective_id=1, has_side_effects=True, vmem_limit_bytes=60 * 1024 * 1024
        ),
        name="tile_step",
    )(
        x, anchor_labels[0], anchor_mask[0], spread, reduce_weight, spatial_weight,
        expand_weight.T, class_weight,
    )
    scale = scale.reshape(())
    return (
        loss.reshape(()),
        small[:mid] * scale,
        spatial * scale,
        (small[mid:] * scale).T,
        wide[:, :, :heads].astype(F32) * scale,
    )


def solution(mesh):
    tiled = P("dp", None, "row", "col")
    return jax.shard_map(
        per_device,
        mesh=mesh,
        in_specs=(tiled, P(), P(), P(), P(), tiled, tiled),
        out_specs=(P(), P(), P(), P(), P()),
        check_vma=False,
    )
```

```python
import functools

import jax
import jax.numpy as jnp
import numpy as np
from jax import lax
from jax.experimental import pallas as pl
from jax.experimental.pallas import tpu as pltpu
from jax.sharding import PartitionSpec as P

A = 9
K = 15
FIRST = (4, 1)
BLOCK = (4, 2)
DLOG = (2, 4)
DSEC = (4, 1)
DFIRST = 16
WIDE = 16
LOG2E = 1.4426950408889634
LN2 = 0.6931471805599453
F32 = jnp.float32
BF16 = jnp.bfloat16
AXES = ("dp", "row", "col")


def dot(a, b):
    return jnp.dot(a, b, preferred_element_type=F32)


def dot_t(a, b):
    return lax.dot_general(a, b, (((1,), (1,)), ((), ())), preferred_element_type=F32)


def step_kernel(
    sizes, heads,
    x_ref, label_ref, mask_ref, spread_ref, wr_ref, spatial_ref, wet_ref, class_ref,
    loss_ref, scale_ref, small_out, spatial_out, class_out,
    first, second, block, dlog, dzero, dsec, dsec_zero, acc_c, acc_s, acc_e, acc_r,
    code_ref, ws_ref, wsb_ref, we_ref, wc_ref, wcb_ref, strips, got,
    stat, stat_slots, big_refs, mid_refs, tail_refs, ssem, rsem, osem,
):
    rows, chans, cols = x_ref.shape
    mid = wr_ref.shape[0]
    outs = wc_ref.shape[2]
    me = {axis: lax.axis_index(axis) for axis in AXES}
    mesh_id = pl.DeviceIdType.MESH
    peers = lambda axis: range(1, sizes[axis])
    used = [0]

    def exists(axis, step):
        return me[axis] < sizes[axis] - 1 if step > 0 else me[axis] > 0

    plane = [
        (d, e) for d in range(sizes["dp"]) for e in range(sizes["col"]) if d or e
    ]
    shift = lambda axis, d: lax.rem(me[axis] + d, sizes[axis])
    across = [{"dp": shift("dp", d), "col": shift("col", e)} for d, e in plane]
    along = [{"row": shift("row", d)} for d in peers("row")]
    place = lambda to: to["dp"] * sizes["col"] + to["col"]

    barrier = pltpu.get_barrier_semaphore()
    for to in across + along:
        pl.semaphore_signal(barrier, inc=1, device_id=to, device_id_type=mesh_id)

    def remote(src, dst, to):
        n = used[0]
        used[0] += 1
        return pltpu.make_async_remote_copy(
            src_ref=src, dst_ref=dst, send_sem=ssem.at[n], recv_sem=rsem.at[n],
            device_id=to, device_id_type=mesh_id,
        )

    def push(src, dst, axis, step):
        copy = remote(src, dst, {axis: me[axis] + step})

        @pl.when(exists(axis, step))
        def _():
            copy.start()

        def finish():
            @pl.when(exists(axis, step))
            def _():
                copy.wait_send()

            @pl.when(exists(axis, -step))
            def _():
                copy.wait_recv()

        return finish

    def settle(copies):
        for copy in copies:
            copy.wait()

    def total_of(slots):
        return sum(slots[j].astype(F32) for j in range(slots.shape[0]))

    def share_all(slots, value, targets, mine):
        slot = slots.at[mine]
        slot[...] = value.astype(slots.dtype)
        copies = [remote(slot, slot, to) for to in targets]
        for copy in copies:
            copy.start()
        return copies

    def reduce_whole(value, plane_slots, row_slots, store):
        copies = share_all(plane_slots, value, across, place(me))
        yield
        settle(copies)
        copies = share_all(row_slots, total_of(plane_slots), along, me["row"])
        yield
        settle(copies)
        store(total_of(row_slots))

    def reduce_split(refs):
        send, full, plane_slots, row_slots = refs
        piece = row_slots.shape[1]
        part = lambda to: pl.ds(pl.multiple_of(place(to) * piece, 16), piece)
        slot = plane_slots.at[place(me)]
        slot[...] = send[part(me), :]
        copies = [remote(send.at[part(to)], slot, to) for to in across]
        for copy in copies:
            copy.start()
        yield
        settle(copies)
        copies = share_all(row_slots, total_of(plane_slots), along, me["row"])
        yield
        settle(copies)
        full[part(me), :] = total_of(row_slots).astype(full.dtype)
        copies = [remote(full.at[part(me)], full.at[part(me)], to) for to in across]
        for copy in copies:
            copy.start()
        yield
        settle(copies)

    def advance(*steps):
        for step in steps:
            next(step, None)

    def loop(steps, body, init=0):
        return lax.fori_loop(0, steps, body, init)

    def cat(ref, at, count, low=None, high=None):
        part = slice(low, high)
        return jnp.concatenate([ref[at + k, part, :] for k in range(count)], axis=1)

    def spread_rows(ref, at, value, low=None, high=None):
        for k in range(value.shape[1] // cols):
            ref[at + k, low:high, :] = value[:, k * cols:(k + 1) * cols]

    def clear_edges(n, field, depth):
        blank = jnp.zeros((depth, cols), BF16)

        @pl.when(jnp.logical_not(exists("row", -1)))
        def _():
            field[0, depth:2 * depth, :] = blank

        @pl.when(jnp.logical_not(exists("row", 1)))
        def _():
            field[rows + 1, depth:2 * depth, :] = blank

        for side in range(2):
            @pl.when(jnp.logical_not(exists("col", 1 if side else -1)))
            def _():
                got[n][side] = blank

    def send_rows(n, field, depth):
        down = push(
            field.at[rows, pl.ds(depth, depth)], field.at[0, pl.ds(depth, depth)], "row", 1
        )
        up = push(
            field.at[1, pl.ds(depth, depth)],
            field.at[rows + 1, pl.ds(depth, depth)], "row", -1,
        )
        return down, up

    def publish(n, field, depth, at, value):
        lane = lax.broadcasted_iota(jnp.int32, (depth, cols), 1) // 2
        for k in range(value.shape[1] // cols):
            row = value[:, k * cols:(k + 1) * cols]
            i = at + k
            field[i, depth:2 * depth, :] = row
            field[i, :depth, :] = pltpu.roll(row, 1, 1)
            field[i, 2 * depth:, :] = pltpu.roll(row, cols - 1, 1)
            strips[n][...] = jnp.where(lane == i, pltpu.roll(row, 2 * i + 1, 1), strips[n][...])

    def send_strip(n, field, depth, held):
        for wait in held:
            wait()
        for i in (0, rows + 1):
            publish(n, field, depth, i, field[i, depth:2 * depth, :])
        right = push(strips[n], got[n].at[0], "col", 1)
        left = push(strips[n], got[n].at[1], "col", -1)
        return right, left

    def widen(n, field, depth, held):
        for wait in held:
            wait()
        lane = lax.broadcasted_iota(jnp.int32, (depth, cols), 1)
        before, after = got[n][0], got[n][1]
        for i in range(rows + 2):
            field[i, :depth, :] = jnp.where(
                lane == 0, pltpu.roll(before, (cols - 2 * i) % cols, 1), field[i, :depth, :]
            )
            field[i, 2 * depth:, :] = jnp.where(
                lane == cols - 1, pltpu.roll(after, (cols - 2 - 2 * i) % cols, 1),
                field[i, 2 * depth:, :],
            )

    def conv(weight, field, at, count):
        return sum(dot(weight(dy), cat(field, at + dy, count)) for dy in range(3))

    def sweep(body, between, size, init=0, halfway=None):
        count, runs = size
        groups = rows // (count * runs)

        def run(j, carry):
            for u in range(runs):
                carry = body((j * runs + u) * count, carry)
            return carry

        carry = loop(2, lambda j, c: run(j * (groups - 1), c), init)
        held = between()
        half = groups // 2 - 1
        carry = loop(half, lambda j, c: run(j + 1, c), carry)
        if halfway is not None:
            halfway()
        return held, loop(groups - 2 - half, lambda j, c: run(j + 1 + half, c), carry)

    fields = [(first, mid), (block, chans), (dlog, outs), (dsec, mid)]
    for n, (field, depth) in enumerate(fields):
        clear_edges(n, field, depth)
        strips[n][...] = jnp.zeros((depth, cols), BF16)
    for ref in (dzero, dsec_zero):
        ref[0] = jnp.zeros(ref.shape[1:], BF16)
        ref[rows + 1] = jnp.zeros(ref.shape[1:], BF16)
    for ref in (acc_e, acc_r, mid_refs[0]) + tuple(refs[0] for refs in big_refs):
        ref[...] = jnp.zeros_like(ref)
    pl.semaphore_wait(barrier, len(across) + len(along))

    def make_first(i, c):
        z = dot(wr_ref[...], cat(x_ref, i, FIRST[0]))
        publish(0, first, mid, i + 1, jnp.maximum(z, 0.0).astype(BF16))
        return c

    held, _ = sweep(make_first, lambda: send_rows(0, first, mid), FIRST)
    for dy in range(3):
        for dx in range(3):
            ws_ref[dy, :, dx * mid:(dx + 1) * mid] = spatial_ref[dy, dx]
            wc_ref[dy, dx, :heads, :] = class_ref[dy, dx]
            wc_ref[dy, dx, heads:, :] = jnp.zeros((outs - heads, chans), BF16)
    for h in range(rows):
        code = jnp.where(mask_ref[:, h, :] > 0, label_ref[:, h, :], 64)
        code_ref[h, :A, :] = code.astype(F32).astype(BF16)
        code_ref[h, A:, :] = jnp.ones((16 - A, cols), BF16)
    held = send_strip(0, first, mid, held)

    def turned(parts):
        size = parts[0].shape[1]
        eye = jnp.where(
            lax.broadcasted_iota(jnp.int32, (size, size), 0)
            == lax.broadcasted_iota(jnp.int32, (size, size), 1), 1.0, 0.0,
        ).astype(BF16)
        return dot_t(eye, jnp.concatenate(parts, axis=0)).astype(BF16)

    we_ref[...] = turned([wet_ref[...]])
    for dy in range(3):
        wsb_ref[dy] = turned([spatial_ref[2 - dy, 2 - dx] for dx in range(3)])
        wcb_ref[dy] = turned([wc_ref[2 - dy, 2 - dx] for dx in range(3)])
    widen(0, first, mid, held)

    def make_block(i, c):
        s = jnp.maximum(conv(lambda dy: ws_ref[dy], first, i, BLOCK[0]), 0.0).astype(BF16)
        spread_rows(second, i, s)
        b = jnp.maximum(cat(x_ref, i, BLOCK[0]).astype(F32) + dot(we_ref[...], s), 0.0)
        publish(1, block, chans, i + 1, b.astype(BF16))
        return c

    held, _ = sweep(make_block, lambda: send_rows(1, block, chans), BLOCK)
    held = send_strip(1, block, chans, held)
    widen(1, block, chans, held)

    def class_rows(dy):
        return jnp.concatenate([wc_ref[dy, dx] for dx in range(3)], axis=1)

    def make_dlog(i, carry):
        total, count = carry
        z = conv(class_rows, block, i, DLOG[0])
        code = cat(code_ref, i, DLOG[0])
        gap = dot(spread_ref[...], code)
        target = gap == 0.0
        alpha = jnp.where(target, 0.25, jnp.where(gap > 32.0, 0.0, 0.75))
        z = z * LOG2E
        u = jnp.where(target, -z, z)
        e = jnp.exp2(-jnp.abs(u))
        soft = jnp.maximum(u, 0.0) + jnp.log2(1.0 + e)
        prob = jnp.exp2(u - soft)
        scaled = alpha * prob * prob
        total = total + jnp.sum(scaled * soft, axis=0, keepdims=True)
        slope = scaled * ((2.0 * LN2 - 2.0 * LN2 * prob) * soft + prob)
        d = jnp.where(target, -slope, slope).astype(BF16)
        publish(2, dlog, outs, i + 1, d)
        spread_rows(dzero, i + 1, d)
        codes = code.astype(F32)
        row = lax.broadcasted_iota(jnp.int32, codes.shape, 0)
        hit = jnp.where((codes > 0.5) & (codes < 32.0) & (row < A), 1.0, 0.0)
        count = count + jnp.sum(hit, axis=0, keepdims=True)
        return total, count

    zero = jnp.zeros((1, DLOG[0] * cols), F32)
    held, (total, count) = sweep(make_dlog, lambda: send_rows(2, dlog, outs), DLOG, (zero, zero))
    fold = lambda v: sum(v[:, k * 128:(k + 1) * 128] for k in range(v.shape[1] // 128))
    stat[0:1, :] = fold(total) * LN2
    stat[1:2, :] = fold(count)
    stat[2:, :] = jnp.zeros((6, 128), F32)

    def keep(value):
        stat[...] = value

    stats = reduce_whole(stat[...], *stat_slots, keep)
    advance(stats)
    held = send_strip(2, dlog, outs, held)

    def weight_sum(acc, grad, field, low, high):
        depth = grad.shape[1]
        acc[...] = jnp.zeros_like(acc)

        def add(i, c):
            at = i * WIDE + 1
            tall = jnp.concatenate([cat(grad, at + 1 - dy, WIDE) for dy in range(3)], axis=0)
            acc[...] += dot_t(tall, cat(field, at, WIDE, low, high))
            return c

        loop(rows // WIDE, add)
        acc[:depth, :] += dot_t(grad[1], field[0, low:high])
        acc[2 * depth:, :] += dot_t(grad[rows], field[rows + 1, low:high])

    bigs = []
    for dx in range(3):
        low, high = dx * chans, (dx + 1) * chans
        weight_sum(acc_c, dzero, block, low, high)
        send = big_refs[dx][0]
        for h in range(chans // 128):
            send[h * 3 * outs:(h + 1) * 3 * outs, :] = acc_c[
                :, h * 128:(h + 1) * 128
            ].astype(BF16)
        bigs.append(reduce_split(big_refs[dx]))
        advance(bigs[dx])
    widen(2, dlog, outs, held)

    def make_dsec(i, c):
        g = conv(lambda dy: wcb_ref[dy], dlog, i, DSEC[0])
        b = cat(block, i + 1, DSEC[0], chans, 2 * chans).astype(F32)
        ds = jnp.where(b > 0.0, g, 0.0).astype(BF16)
        s = cat(second, i, DSEC[0])
        acc_e[...] += dot_t(s, ds)
        h = dot(wet_ref[...], ds)
        d = jnp.where(s.astype(F32) > 0.0, h, 0.0).astype(BF16)
        publish(3, dsec, mid, i + 1, d)
        spread_rows(dsec_zero, i + 1, d)
        return c

    def after_edges():
        sent = send_rows(3, dsec, mid)
        advance(bigs[0], stats)
        return sent

    held, _ = sweep(make_dsec, after_edges, DSEC, halfway=lambda: advance(*bigs[1:]))
    held = send_strip(3, dsec, mid, held)
    advance(bigs[0], stats)
    weight_sum(acc_s, dsec_zero, first, 0, 3 * mid)
    mid_send, mid_full = mid_refs[:2]
    mid_send[:mid, :] = acc_e[...].astype(BF16)
    mid_send[mid:4 * mid, :3 * mid] = acc_s[...].astype(BF16)
    middle = reduce_split(mid_refs)
    advance(middle)
    advance(bigs[1])
    widen(3, dsec, mid, held)
    advance(bigs[2])

    def make_dfirst(i, c):
        g = conv(lambda dy: wsb_ref[dy], dsec, i, DFIRST)
        f = cat(first, i + 1, DFIRST, mid, 2 * mid).astype(F32)
        df = jnp.where(f > 0.0, g, 0.0).astype(BF16)
        acc_r[...] += dot_t(df, cat(x_ref, i, DFIRST))
        return c

    loop(rows // DFIRST, lambda j, c: make_dfirst(j * DFIRST, c))

    def place_tail(value):
        small_out[:mid, :] = value

    tail = reduce_whole(acc_r[...], *tail_refs, place_tail)
    advance(tail)
    scale = 1.0 / jnp.sum(stat[1:2, :], axis=1, keepdims=True)
    scale_ref[...] = scale
    loss_ref[...] = jnp.sum(stat[0:1, :], axis=1, keepdims=True) * scale
    advance(middle)
    advance(tail)
    outgoing = []
    for dx in range(3):
        advance(bigs[dx])
        for h in range(chans // 128):
            for dy in range(3):
                at = (3 * h + dy) * outs
                outgoing.append(pltpu.make_async_copy(
                    big_refs[dx][1].at[pl.ds(at, outs)],
                    class_out.at[dy, dx, :, pl.ds(h * 128, 128)], osem.at[len(outgoing)],
                ))
                outgoing[-1].start()
    advance(middle)
    advance(middle)
    small_out[mid:, :] = mid_full[:mid, :].astype(F32)
    for dy in range(3):
        part = mid_full[(dy + 1) * mid:(dy + 2) * mid, :].astype(F32)
        for dx in range(3):
            spatial_out[dy, dx] = part[:, dx * mid:(dx + 1) * mid]
    advance(tail)
    for copy in outgoing:
        copy.wait()


def per_device(
    inputs, reduce_weight, spatial_weight, expand_weight, class_weight, anchor_labels, anchor_mask
):
    tiles, chans, rows, cols = inputs.shape
    assert tiles == 1
    mid = reduce_weight.shape[0]
    heads = class_weight.shape[2]
    outs = -(-heads // 16) * 16
    sizes = {axis: lax.axis_size(axis) for axis in AXES}

    x = inputs[0].transpose(1, 0, 2)

    spread = np.zeros((outs, 16), np.float32)
    spread[np.arange(heads), np.arange(heads) // K] = 1.0
    spread[np.arange(heads), A] = -1.0 - np.arange(heads) % K
    spread[heads:, A] = 64.0
    spread = jnp.asarray(spread, BF16)

    depths = (mid, chans, outs, mid)
    across = sizes["dp"] * sizes["col"]

    def split_refs(need, wide):
        piece = -(-need // (16 * across)) * 16
        full = pltpu.VMEM((piece * across, wide), BF16)
        return [full, full] + [
            pltpu.VMEM((count, piece, wide), BF16) for count in (across, sizes["row"])
        ]

    def whole_refs(shape, kind):
        return [pltpu.VMEM((count,) + shape, kind) for count in (across, sizes["row"])]

    copies = 16 + 6 * (across - 1) + 4 * (across - 1) + 6 * (sizes["row"] - 1)
    outputs = [
        ((1, 1), F32), ((1, 1), F32), ((2 * mid, chans), F32), ((3, 3, mid, mid), F32),
        ((3, 3, outs, chans), BF16),
    ]

    loss, scale, small, spatial, wide = pl.pallas_call(
        functools.partial(step_kernel, sizes, heads),
        out_shape=[jax.ShapeDtypeStruct(*output) for output in outputs],
        in_specs=[pl.BlockSpec(memory_space=pltpu.VMEM)] * 8,
        out_specs=[pl.BlockSpec(memory_space=pltpu.VMEM)] * 4
        + [pl.BlockSpec(memory_space=pl.ANY)],
        scratch_shapes=[
            pltpu.VMEM((rows + 2, 3 * mid, cols), BF16),
            pltpu.VMEM((rows, mid, cols), BF16),
            pltpu.VMEM((rows + 2, 3 * chans, cols), BF16),
            pltpu.VMEM((rows + 2, 3 * outs, cols), BF16),
            pltpu.VMEM((rows + 2, outs, cols), BF16),
            pltpu.VMEM((rows + 2, 3 * mid, cols), BF16),
            pltpu.VMEM((rows + 2, mid, cols), BF16),
            pltpu.VMEM((3 * outs, chans), F32),
            pltpu.VMEM((3 * mid, 3 * mid), F32),
            pltpu.VMEM((mid, chans), F32),
            pltpu.VMEM((mid, chans), F32),
            pltpu.VMEM((rows, 16, cols), BF16),
            pltpu.VMEM((3, mid, 3 * mid), BF16),
            pltpu.VMEM((3, mid, 3 * mid), BF16),
            pltpu.VMEM((chans, mid), BF16),
            pltpu.VMEM((3, 3, outs, chans), BF16),
            pltpu.VMEM((3, chans, 3 * outs), BF16),
            [pltpu.VMEM((depth, cols), BF16) for depth in depths],
            [pltpu.VMEM((2, depth, cols), BF16) for depth in depths],
            pltpu.VMEM((8, 128), F32),
            whole_refs((8, 128), F32),
            [split_refs(3 * outs * chans // 128, 128) for _ in range(3)],
            split_refs(4 * mid, chans),
            whole_refs((mid, chans), BF16),
            pltpu.SemaphoreType.DMA((copies,)),
            pltpu.SemaphoreType.DMA((copies,)),
            pltpu.SemaphoreType.DMA((9 * chans // 128,)),
        ],
        compiler_params=pltpu.CompilerParams(
            collective_id=1, has_side_effects=True, vmem_limit_bytes=36 * 1024 * 1024
        ),
        name="tile_step",
    )(
        x, anchor_labels[0], anchor_mask[0], spread, reduce_weight, spatial_weight,
        expand_weight.T, class_weight,
    )
    scale = scale.reshape(())
    return (
        loss.reshape(()),
        small[:mid] * scale,
        spatial * scale,
        (small[mid:] * scale).T,
        wide[:, :, :heads].astype(F32) * scale,
    )


def solution(mesh):
    tiled = P("dp", None, "row", "col")
    return jax.shard_map(
        per_device,
        mesh=mesh,
        in_specs=(tiled, P(), P(), P(), P(), tiled, tiled),
        out_specs=(P(), P(), P(), P(), P()),
        check_vma=False,
    )
```

```python
import functools

import jax
import jax.numpy as jnp
import numpy as np
from jax import lax
from jax.experimental import pallas as pl
from jax.experimental.pallas import tpu as pltpu
from jax.sharding import PartitionSpec as P

A = 9
K = 15
FIRST = (4, 1)
BLOCK = (4, 2)
DLOG = (2, 4)
DSEC = (4, 1)
DFIRST = 16
WIDE = 16
LOG2E = 1.4426950408889634
LN2 = 0.6931471805599453
F32 = jnp.float32
BF16 = jnp.bfloat16
AXES = ("dp", "row", "col")


def dot(a, b):
    return jnp.dot(a, b, preferred_element_type=F32)


def dot_t(a, b):
    return lax.dot_general(a, b, (((1,), (1,)), ((), ())), preferred_element_type=F32)


def step_kernel(
    sizes, heads,
    x_ref, label_ref, mask_ref, spread_ref, wr_ref, spatial_ref, wet_ref, class_ref,
    small_out, spatial_out, class_out,
    first, second, block, dlog, dzero, dsec, dsec_zero, acc_c, acc_s, acc_e, acc_r,
    code_ref, ws_ref, wsb_ref, we_ref, wc_ref, wcb_ref, strips, got,
    stat, stat_slots, big_refs, mid_refs, tail_refs, ssem, rsem,
):
    rows, chans, cols = x_ref.shape
    mid = wr_ref.shape[0]
    outs = wc_ref.shape[2]
    me = {axis: lax.axis_index(axis) for axis in AXES}
    mesh_id = pl.DeviceIdType.MESH
    peers = lambda axis: range(1, sizes[axis])
    used = [0]

    def exists(axis, step):
        return me[axis] < sizes[axis] - 1 if step > 0 else me[axis] > 0

    plane = [
        (d, e) for d in range(sizes["dp"]) for e in range(sizes["col"]) if d or e
    ]
    shift = lambda axis, d: lax.rem(me[axis] + d, sizes[axis])
    across = [{"dp": shift("dp", d), "col": shift("col", e)} for d, e in plane]
    along = [{"row": shift("row", d)} for d in peers("row")]
    place = lambda to: to["dp"] * sizes["col"] + to["col"]

    barrier = pltpu.get_barrier_semaphore()
    for to in across + along:
        pl.semaphore_signal(barrier, inc=1, device_id=to, device_id_type=mesh_id)

    def remote(src, dst, to):
        n = used[0]
        used[0] += 1
        return pltpu.make_async_remote_copy(
            src_ref=src, dst_ref=dst, send_sem=ssem.at[n], recv_sem=rsem.at[n],
            device_id=to, device_id_type=mesh_id,
        )

    def push(src, dst, axis, step):
        copy = remote(src, dst, {axis: me[axis] + step})

        @pl.when(exists(axis, step))
        def _():
            copy.start()

        def finish():
            @pl.when(exists(axis, step))
            def _():
                copy.wait_send()

            @pl.when(exists(axis, -step))
            def _():
                copy.wait_recv()

        return finish

    def settle(copies):
        for copy in copies:
            copy.wait()

    def total_of(slots):
        return sum(slots[j].astype(F32) for j in range(slots.shape[0]))

    def share_all(slots, value, targets, mine):
        slot = slots.at[mine]
        slot[...] = value.astype(slots.dtype)
        copies = [remote(slot, slot, to) for to in targets]
        for copy in copies:
            copy.start()
        return copies

    def reduce_whole(value, plane_slots, row_slots, store):
        copies = share_all(row_slots, value, along, me["row"])
        yield
        settle(copies)
        copies = share_all(plane_slots, total_of(row_slots), across, place(me))
        yield
        settle(copies)
        store(total_of(plane_slots))

    def reduce_split(refs):
        send, full, plane_slots, row_slots = refs
        piece = row_slots.shape[1]
        part = lambda to: pl.ds(pl.multiple_of(place(to) * piece, 16), piece)
        slot = plane_slots.at[place(me)]
        slot[...] = send[part(me), :]
        copies = [remote(send.at[part(to)], slot, to) for to in across]
        for copy in copies:
            copy.start()
        yield
        settle(copies)
        copies = share_all(row_slots, total_of(plane_slots), along, me["row"])
        yield
        settle(copies)
        full[part(me), :] = total_of(row_slots).astype(full.dtype)
        copies = [remote(full.at[part(me)], full.at[part(me)], to) for to in across]
        for copy in copies:
            copy.start()
        yield
        settle(copies)

    def advance(*steps):
        for step in steps:
            next(step, None)

    def loop(steps, body, init=0):
        return lax.fori_loop(0, steps, body, init)

    def cat(ref, at, count, low=None, high=None):
        part = slice(low, high)
        return jnp.concatenate([ref[at + k, part, :] for k in range(count)], axis=1)

    def spread_rows(ref, at, value, low=None, high=None):
        for k in range(value.shape[1] // cols):
            ref[at + k, low:high, :] = value[:, k * cols:(k + 1) * cols]

    def clear_edges(n, field, depth):
        blank = jnp.zeros((depth, cols), BF16)

        @pl.when(jnp.logical_not(exists("row", -1)))
        def _():
            field[0, depth:2 * depth, :] = blank

        @pl.when(jnp.logical_not(exists("row", 1)))
        def _():
            field[rows + 1, depth:2 * depth, :] = blank

        for side in range(2):
            @pl.when(jnp.logical_not(exists("col", 1 if side else -1)))
            def _():
                got[n][side] = blank

    def send_rows(n, field, depth):
        down = push(
            field.at[rows, pl.ds(depth, depth)], field.at[0, pl.ds(depth, depth)], "row", 1
        )
        up = push(
            field.at[1, pl.ds(depth, depth)],
            field.at[rows + 1, pl.ds(depth, depth)], "row", -1,
        )
        return down, up

    def publish(n, field, depth, at, value):
        lane = lax.broadcasted_iota(jnp.int32, (depth, cols), 1) // 2
        for k in range(value.shape[1] // cols):
            row = value[:, k * cols:(k + 1) * cols]
            i = at + k
            field[i, depth:2 * depth, :] = row
            field[i, :depth, :] = pltpu.roll(row, 1, 1)
            field[i, 2 * depth:, :] = pltpu.roll(row, cols - 1, 1)
            strips[n][...] = jnp.where(lane == i, pltpu.roll(row, 2 * i + 1, 1), strips[n][...])

    def send_strip(n, field, depth, held):
        for wait in held:
            wait()
        for i in (0, rows + 1):
            publish(n, field, depth, i, field[i, depth:2 * depth, :])
        right = push(strips[n], got[n].at[0], "col", 1)
        left = push(strips[n], got[n].at[1], "col", -1)
        return right, left

    def widen(n, field, depth, held):
        for wait in held:
            wait()
        lane = lax.broadcasted_iota(jnp.int32, (depth, cols), 1)
        before, after = got[n][0], got[n][1]
        for i in range(rows + 2):
            field[i, :depth, :] = jnp.where(
                lane == 0, pltpu.roll(before, (cols - 2 * i) % cols, 1), field[i, :depth, :]
            )
            field[i, 2 * depth:, :] = jnp.where(
                lane == cols - 1, pltpu.roll(after, (cols - 2 - 2 * i) % cols, 1),
                field[i, 2 * depth:, :],
            )

    def conv(weight, field, at, count):
        return sum(dot(weight(dy), cat(field, at + dy, count)) for dy in range(3))

    def sweep(body, between, size, init=0, halfway=None):
        count, runs = size
        groups = rows // (count * runs)

        def run(j, carry):
            for u in range(runs):
                carry = body((j * runs + u) * count, carry)
            return carry

        carry = loop(2, lambda j, c: run(j * (groups - 1), c), init)
        held = between()
        half = groups // 2 - 1
        carry = loop(half, lambda j, c: run(j + 1, c), carry)
        if halfway is not None:
            halfway()
        return held, loop(groups - 2 - half, lambda j, c: run(j + 1 + half, c), carry)

    fields = [(first, mid), (block, chans), (dlog, outs), (dsec, mid)]
    for n, (field, depth) in enumerate(fields):
        clear_edges(n, field, depth)
        strips[n][...] = jnp.zeros((depth, cols), BF16)
    for ref in (dzero, dsec_zero):
        ref[0] = jnp.zeros(ref.shape[1:], BF16)
        ref[rows + 1] = jnp.zeros(ref.shape[1:], BF16)
    for ref in (acc_e, acc_r, mid_refs[0]) + tuple(refs[0] for refs in big_refs):
        ref[...] = jnp.zeros_like(ref)
    pl.semaphore_wait(barrier, len(across) + len(along))

    def make_first(i, c):
        z = dot(wr_ref[...], cat(x_ref, i, FIRST[0]))
        publish(0, first, mid, i + 1, jnp.maximum(z, 0.0).astype(BF16))
        return c

    held, _ = sweep(make_first, lambda: send_rows(0, first, mid), FIRST)
    for dy in range(3):
        for dx in range(3):
            ws_ref[dy, :, dx * mid:(dx + 1) * mid] = spatial_ref[dy, dx]
            wc_ref[dy, dx, :heads, :] = class_ref[dy, dx]
            wc_ref[dy, dx, heads:, :] = jnp.zeros((outs - heads, chans), BF16)
    for h in range(rows):
        code = jnp.where(mask_ref[:, h, :] > 0, label_ref[:, h, :], 64)
        code_ref[h, :A, :] = code.astype(F32).astype(BF16)
        code_ref[h, A:, :] = jnp.ones((16 - A, cols), BF16)
    held = send_strip(0, first, mid, held)

    def turned(parts):
        size = parts[0].shape[1]
        eye = jnp.where(
            lax.broadcasted_iota(jnp.int32, (size, size), 0)
            == lax.broadcasted_iota(jnp.int32, (size, size), 1), 1.0, 0.0,
        ).astype(BF16)
        return dot_t(eye, jnp.concatenate(parts, axis=0)).astype(BF16)

    we_ref[...] = turned([wet_ref[...]])
    for dy in range(3):
        wsb_ref[dy] = turned([spatial_ref[2 - dy, 2 - dx] for dx in range(3)])
        wcb_ref[dy] = turned([wc_ref[2 - dy, 2 - dx] for dx in range(3)])
    widen(0, first, mid, held)

    def make_block(i, c):
        s = jnp.maximum(conv(lambda dy: ws_ref[dy], first, i, BLOCK[0]), 0.0).astype(BF16)
        spread_rows(second, i, s)
        b = jnp.maximum(cat(x_ref, i, BLOCK[0]).astype(F32) + dot(we_ref[...], s), 0.0)
        publish(1, block, chans, i + 1, b.astype(BF16))
        return c

    held, _ = sweep(make_block, lambda: send_rows(1, block, chans), BLOCK)
    held = send_strip(1, block, chans, held)
    widen(1, block, chans, held)

    def class_rows(dy):
        return jnp.concatenate([wc_ref[dy, dx] for dx in range(3)], axis=1)

    def make_dlog(i, carry):
        total, count = carry
        z = conv(class_rows, block, i, DLOG[0])
        code = cat(code_ref, i, DLOG[0])
        gap = dot(spread_ref[...], code)
        target = gap == 0.0
        alpha = jnp.where(target, 0.25, jnp.where(gap > 32.0, 0.0, 0.75))
        z = z * LOG2E
        u = jnp.where(target, -z, z)
        e = jnp.exp2(-jnp.abs(u))
        soft = jnp.maximum(u, 0.0) + jnp.log2(1.0 + e)
        prob = jnp.exp2(u - soft)
        scaled = alpha * prob * prob
        total = total + jnp.sum(scaled * soft, axis=0, keepdims=True)
        slope = scaled * ((2.0 * LN2 - 2.0 * LN2 * prob) * soft + prob)
        d = jnp.where(target, -slope, slope).astype(BF16)
        publish(2, dlog, outs, i + 1, d)
        spread_rows(dzero, i + 1, d)
        codes = code.astype(F32)
        row = lax.broadcasted_iota(jnp.int32, codes.shape, 0)
        hit = jnp.where((codes > 0.5) & (codes < 32.0) & (row < A), 1.0, 0.0)
        count = count + jnp.sum(hit, axis=0, keepdims=True)
        return total, count

    zero = jnp.zeros((1, DLOG[0] * cols), F32)
    held, (total, count) = sweep(make_dlog, lambda: send_rows(2, dlog, outs), DLOG, (zero, zero))
    fold = lambda v: sum(v[:, k * 128:(k + 1) * 128] for k in range(v.shape[1] // 128))
    stat[0:1, :] = fold(total) * LN2
    stat[1:2, :] = fold(count)
    stat[2:, :] = jnp.zeros((6, 128), F32)

    def keep(value):
        stat[...] = value

    stats = reduce_whole(stat[...], *stat_slots, keep)
    advance(stats)
    held = send_strip(2, dlog, outs, held)

    def weight_sum(acc, grad, field, low, high):
        depth = grad.shape[1]
        acc[...] = jnp.zeros_like(acc)

        def add(i, c):
            at = i * WIDE + 1
            tall = jnp.concatenate([cat(grad, at + 1 - dy, WIDE) for dy in range(3)], axis=0)
            acc[...] += dot_t(tall, cat(field, at, WIDE, low, high))
            return c

        loop(rows // WIDE, add)
        acc[:depth, :] += dot_t(grad[1], field[0, low:high])
        acc[2 * depth:, :] += dot_t(grad[rows], field[rows + 1, low:high])

    bigs = []
    for dx in range(3):
        low, high = dx * chans, (dx + 1) * chans
        weight_sum(acc_c, dzero, block, low, high)
        send = big_refs[dx][0]
        for h in range(chans // 128):
            send[h * 3 * outs:(h + 1) * 3 * outs, :] = acc_c[
                :, h * 128:(h + 1) * 128
            ].astype(BF16)
        bigs.append(reduce_split(big_refs[dx]))
        advance(bigs[dx])
    widen(2, dlog, outs, held)

    def make_dsec(i, c):
        g = conv(lambda dy: wcb_ref[dy], dlog, i, DSEC[0])
        b = cat(block, i + 1, DSEC[0], chans, 2 * chans).astype(F32)
        ds = jnp.where(b > 0.0, g, 0.0).astype(BF16)
        s = cat(second, i, DSEC[0])
        acc_e[...] += dot_t(s, ds)
        h = dot(wet_ref[...], ds)
        d = jnp.where(s.astype(F32) > 0.0, h, 0.0).astype(BF16)
        publish(3, dsec, mid, i + 1, d)
        spread_rows(dsec_zero, i + 1, d)
        return c

    def after_edges():
        sent = send_rows(3, dsec, mid)
        advance(bigs[0], stats)
        return sent

    held, _ = sweep(make_dsec, after_edges, DSEC, halfway=lambda: advance(*bigs[1:]))
    held = send_strip(3, dsec, mid, held)
    advance(bigs[0], stats)
    weight_sum(acc_s, dsec_zero, first, 0, 3 * mid)
    mid_send, mid_full = mid_refs[:2]
    mid_send[:mid, :] = acc_e[...].astype(BF16)
    mid_send[mid:4 * mid, :3 * mid] = acc_s[...].astype(BF16)
    middle = reduce_split(mid_refs)
    advance(middle)
    advance(bigs[1])
    widen(3, dsec, mid, held)
    advance(bigs[2])

    def make_dfirst(i, c):
        g = conv(lambda dy: wsb_ref[dy], dsec, i, DFIRST)
        f = cat(first, i + 1, DFIRST, mid, 2 * mid).astype(F32)
        df = jnp.where(f > 0.0, g, 0.0).astype(BF16)
        acc_r[...] += dot_t(df, cat(x_ref, i, DFIRST))
        return c

    loop(rows // DFIRST, lambda j, c: make_dfirst(j * DFIRST, c))

    def place_tail(value):
        small_out[:mid, :] = value

    tail = reduce_whole(acc_r[...], *tail_refs, place_tail)
    advance(tail)
    scale = 1.0 / jnp.sum(stat[1:2, :], axis=1, keepdims=True)
    loss = jnp.sum(stat[0:1, :], axis=1, keepdims=True) * scale
    advance(middle)
    advance(tail)
    for dx in range(3):
        advance(bigs[dx])
        for h in range(chans // 128):
            for dy in range(3):
                at = (3 * h + dy) * outs
                class_out[dy, dx, :, h * 128:(h + 1) * 128] = (
                    big_refs[dx][1][at:at + outs, :].astype(F32) * scale
                )
    advance(middle)
    advance(middle)
    small_out[mid:2 * mid, :] = mid_full[:mid, :].astype(F32) * scale
    small_out[2 * mid:, :] = jnp.broadcast_to(loss, (8, chans))
    for dy in range(3):
        part = mid_full[(dy + 1) * mid:(dy + 2) * mid, :].astype(F32) * scale
        for dx in range(3):
            spatial_out[dy, dx] = part[:, dx * mid:(dx + 1) * mid]
    spatial_out[3] = jnp.zeros(spatial_out.shape[1:], F32)
    advance(tail)
    small_out[:mid, :] = small_out[:mid, :] * scale


def per_device(
    inputs, reduce_weight, spatial_weight, expand_weight, class_weight, anchor_labels, anchor_mask
):
    tiles, chans, rows, cols = inputs.shape
    assert tiles == 1
    mid = reduce_weight.shape[0]
    heads = class_weight.shape[2]
    outs = -(-heads // 16) * 16
    sizes = {axis: lax.axis_size(axis) for axis in AXES}

    x = inputs[0].transpose(1, 0, 2)

    spread = np.zeros((outs, 16), np.float32)
    spread[np.arange(heads), np.arange(heads) // K] = 1.0
    spread[np.arange(heads), A] = -1.0 - np.arange(heads) % K
    spread[heads:, A] = 64.0
    spread = jnp.asarray(spread, BF16)

    depths = (mid, chans, outs, mid)
    across = sizes["dp"] * sizes["col"]

    def split_refs(need, wide):
        piece = -(-need // (16 * across)) * 16
        full = pltpu.VMEM((piece * across, wide), BF16)
        return [full, full] + [
            pltpu.VMEM((count, piece, wide), BF16) for count in (across, sizes["row"])
        ]

    def whole_refs(shape, kind):
        return [pltpu.VMEM((count,) + shape, kind) for count in (across, sizes["row"])]

    copies = 16 + 6 * (across - 1) + 4 * (across - 1) + 6 * (sizes["row"] - 1)
    outputs = [
        ((2 * mid + 8, chans), F32), ((4, 3, mid, mid), F32), ((3, 3, outs, chans), F32)
    ]

    small, spatial, wide = pl.pallas_call(
        functools.partial(step_kernel, sizes, heads),
        out_shape=[jax.ShapeDtypeStruct(*output) for output in outputs],
        in_specs=[pl.BlockSpec(memory_space=pltpu.VMEM)] * 8,
        out_specs=[pl.BlockSpec(memory_space=pltpu.VMEM)] * 3,
        scratch_shapes=[
            pltpu.VMEM((rows + 2, 3 * mid, cols), BF16),
            pltpu.VMEM((rows, mid, cols), BF16),
            pltpu.VMEM((rows + 2, 3 * chans, cols), BF16),
            pltpu.VMEM((rows + 2, 3 * outs, cols), BF16),
            pltpu.VMEM((rows + 2, outs, cols), BF16),
            pltpu.VMEM((rows + 2, 3 * mid, cols), BF16),
            pltpu.VMEM((rows + 2, mid, cols), BF16),
            pltpu.VMEM((3 * outs, chans), F32),
            pltpu.VMEM((3 * mid, 3 * mid), F32),
            pltpu.VMEM((mid, chans), F32),
            pltpu.VMEM((mid, chans), F32),
            pltpu.VMEM((rows, 16, cols), BF16),
            pltpu.VMEM((3, mid, 3 * mid), BF16),
            pltpu.VMEM((3, mid, 3 * mid), BF16),
            pltpu.VMEM((chans, mid), BF16),
            pltpu.VMEM((3, 3, outs, chans), BF16),
            pltpu.VMEM((3, chans, 3 * outs), BF16),
            [pltpu.VMEM((depth, cols), BF16) for depth in depths],
            [pltpu.VMEM((2, depth, cols), BF16) for depth in depths],
            pltpu.VMEM((8, 128), F32),
            whole_refs((8, 128), F32),
            [split_refs(3 * outs * chans // 128, 128) for _ in range(3)],
            split_refs(4 * mid, chans),
            whole_refs((mid, chans), BF16),
            pltpu.SemaphoreType.DMA((copies,)),
            pltpu.SemaphoreType.DMA((copies,)),
        ],
        compiler_params=pltpu.CompilerParams(
            collective_id=1, has_side_effects=True, vmem_limit_bytes=36 * 1024 * 1024
        ),
        name="tile_step",
    )(
        x, anchor_labels[0], anchor_mask[0], spread, reduce_weight, spatial_weight,
        expand_weight.T, class_weight,
    )
    return (
        small[2 * mid, 0], small[:mid], spatial[:3], small[mid:2 * mid].T, wide[:, :, :heads]
    )


def solution(mesh):
    tiled = P("dp", None, "row", "col")
    return jax.shard_map(
        per_device,
        mesh=mesh,
        in_specs=(tiled, P(), P(), P(), P(), tiled, tiled),
        out_specs=(P(), P(), P(), P(), P()),
        check_vma=False,
    )
```

```python
import functools

import jax
import jax.numpy as jnp
import numpy as np
from jax import lax
from jax.experimental import pallas as pl
from jax.experimental.pallas import tpu as pltpu
from jax.sharding import PartitionSpec as P

A = 9
K = 15
FIRST = (4, 1)
BLOCK = (4, 2)
DLOG = (2, 4)
DSEC = (4, 1)
DFIRST = 16
WIDE = 16
LOG2E = 1.4426950408889634
LN2 = 0.6931471805599453
F32 = jnp.float32
BF16 = jnp.bfloat16
AXES = ("dp", "row", "col")


def dot(a, b):
    return jnp.dot(a, b, preferred_element_type=F32)


def dot_t(a, b):
    return lax.dot_general(a, b, (((1,), (1,)), ((), ())), preferred_element_type=F32)


def step_kernel(
    sizes, heads,
    x_ref, label_ref, mask_ref, spread_ref, wr_ref, spatial_ref, wet_ref, class_ref,
    small_out, spatial_out, class_out,
    first, second, block, dlog, dzero, dsec, dsec_zero, acc_c, acc_s, acc_e, acc_r,
    code_ref, ws_ref, wsb_ref, we_ref, wc_ref, wcb_ref, strips, got,
    stat, stat_slots, big_refs, mid_refs, tail_refs, ssem, rsem,
):
    rows, chans, cols = x_ref.shape
    mid = wr_ref.shape[0]
    outs = wc_ref.shape[2]
    me = {axis: lax.axis_index(axis) for axis in AXES}
    mesh_id = pl.DeviceIdType.MESH
    peers = lambda axis: range(1, sizes[axis])
    used = [0]

    def exists(axis, step):
        return me[axis] < sizes[axis] - 1 if step > 0 else me[axis] > 0

    plane = [
        (d, e) for d in range(sizes["dp"]) for e in range(sizes["col"]) if d or e
    ]
    shift = lambda axis, d: lax.rem(me[axis] + d, sizes[axis])
    across = [{"dp": shift("dp", d), "col": shift("col", e)} for d, e in plane]
    along = [{"row": shift("row", d)} for d in peers("row")]
    place = lambda to: to["dp"] * sizes["col"] + to["col"]

    barrier = pltpu.get_barrier_semaphore()
    for to in across + along:
        pl.semaphore_signal(barrier, inc=1, device_id=to, device_id_type=mesh_id)

    def remote(src, dst, to):
        n = used[0]
        used[0] += 1
        return pltpu.make_async_remote_copy(
            src_ref=src, dst_ref=dst, send_sem=ssem.at[n], recv_sem=rsem.at[n],
            device_id=to, device_id_type=mesh_id,
        )

    def push(src, dst, axis, step):
        copy = remote(src, dst, {axis: me[axis] + step})

        @pl.when(exists(axis, step))
        def _():
            copy.start()

        def finish():
            @pl.when(exists(axis, step))
            def _():
                copy.wait_send()

            @pl.when(exists(axis, -step))
            def _():
                copy.wait_recv()

        return finish

    def settle(copies):
        for copy in copies:
            copy.wait()

    def total_of(slots):
        return sum(slots[j].astype(F32) for j in range(slots.shape[0]))

    def share_all(slots, value, targets, mine):
        slot = slots.at[mine]
        slot[...] = value.astype(slots.dtype)
        copies = [remote(slot, slot, to) for to in targets]
        for copy in copies:
            copy.start()
        return copies

    def reduce_whole(value, plane_slots, row_slots, store):
        copies = share_all(row_slots, value, along, me["row"])
        yield
        settle(copies)
        copies = share_all(plane_slots, total_of(row_slots), across, place(me))
        yield
        settle(copies)
        store(total_of(plane_slots))

    def reduce_split(refs):
        send, full, plane_slots, row_slots = refs
        piece = row_slots.shape[1]
        part = lambda to: pl.ds(pl.multiple_of(place(to) * piece, 16), piece)
        slot = plane_slots.at[place(me)]
        slot[...] = send[part(me), :]
        copies = [remote(send.at[part(to)], slot, to) for to in across]
        for copy in copies:
            copy.start()
        yield
        settle(copies)
        copies = share_all(row_slots, total_of(plane_slots), along, me["row"])
        yield
        settle(copies)
        full[part(me), :] = total_of(row_slots).astype(full.dtype)
        copies = [remote(full.at[part(me)], full.at[part(me)], to) for to in across]
        for copy in copies:
            copy.start()
        yield
        settle(copies)

    def advance(*steps):
        for step in steps:
            next(step, None)

    def loop(steps, body, init=0):
        return lax.fori_loop(0, steps, body, init)

    def cat(ref, at, count, low=None, high=None):
        part = slice(low, high)
        return jnp.concatenate([ref[at + k, part, :] for k in range(count)], axis=1)

    def spread_rows(ref, at, value, low=None, high=None):
        for k in range(value.shape[1] // cols):
            ref[at + k, low:high, :] = value[:, k * cols:(k + 1) * cols]

    def clear_edges(n, field, depth):
        blank = jnp.zeros((depth, cols), BF16)

        @pl.when(jnp.logical_not(exists("row", -1)))
        def _():
            field[0, depth:2 * depth, :] = blank

        @pl.when(jnp.logical_not(exists("row", 1)))
        def _():
            field[rows + 1, depth:2 * depth, :] = blank

        for side in range(2):
            @pl.when(jnp.logical_not(exists("col", 1 if side else -1)))
            def _():
                got[n][side] = blank

    def send_rows(n, field, depth):
        down = push(
            field.at[rows, pl.ds(depth, depth)], field.at[0, pl.ds(depth, depth)], "row", 1
        )
        up = push(
            field.at[1, pl.ds(depth, depth)],
            field.at[rows + 1, pl.ds(depth, depth)], "row", -1,
        )
        return down, up

    def publish(n, field, depth, at, value):
        lane = lax.broadcasted_iota(jnp.int32, (depth, cols), 1) // 2
        for k in range(value.shape[1] // cols):
            row = value[:, k * cols:(k + 1) * cols]
            i = at + k
            field[i, depth:2 * depth, :] = row
            field[i, :depth, :] = pltpu.roll(row, 1, 1)
            field[i, 2 * depth:, :] = pltpu.roll(row, cols - 1, 1)
            strips[n][...] = jnp.where(lane == i, pltpu.roll(row, 2 * i + 1, 1), strips[n][...])

    def send_strip(n, field, depth, held):
        for wait in held:
            wait()
        for i in (0, rows + 1):
            publish(n, field, depth, i, field[i, depth:2 * depth, :])
        right = push(strips[n], got[n].at[0], "col", 1)
        left = push(strips[n], got[n].at[1], "col", -1)
        return right, left

    def widen(n, field, depth, held):
        for wait in held:
            wait()
        lane = lax.broadcasted_iota(jnp.int32, (depth, cols), 1)
        both = jnp.where(
            lane % 2 == 1, pltpu.roll(got[n][0], 1, 1), pltpu.roll(got[n][1], cols - 1, 1)
        )
        for i in range(rows + 2):
            ends = pltpu.roll(both, (cols - 1 - 2 * i) % cols, 1)
            field[i, :depth, :] = jnp.where(lane == 0, ends, field[i, :depth, :])
            field[i, 2 * depth:, :] = jnp.where(lane == cols - 1, ends, field[i, 2 * depth:, :])

    def conv(weight, field, at, count):
        return sum(dot(weight(dy), cat(field, at + dy, count)) for dy in range(3))

    def sweep(body, between, size, init=0, halfway=None):
        count, runs = size
        groups = rows // (count * runs)

        def run(j, carry):
            for u in range(runs):
                carry = body((j * runs + u) * count, carry)
            return carry

        carry = loop(2, lambda j, c: run(j * (groups - 1), c), init)
        held = between()
        half = groups // 2 - 1
        carry = loop(half, lambda j, c: run(j + 1, c), carry)
        if halfway is not None:
            halfway()
        return held, loop(groups - 2 - half, lambda j, c: run(j + 1 + half, c), carry)

    fields = [(first, mid), (block, chans), (dlog, outs), (dsec, mid)]
    for n, (field, depth) in enumerate(fields):
        clear_edges(n, field, depth)
        strips[n][...] = jnp.zeros((depth, cols), BF16)
    for ref in (dzero, dsec_zero):
        ref[0] = jnp.zeros(ref.shape[1:], BF16)
        ref[rows + 1] = jnp.zeros(ref.shape[1:], BF16)
    for ref in (acc_e, acc_r, mid_refs[0]) + tuple(refs[0] for refs in big_refs):
        ref[...] = jnp.zeros_like(ref)
    pl.semaphore_wait(barrier, len(across) + len(along))

    def make_first(i, c):
        z = dot(wr_ref[...], cat(x_ref, i, FIRST[0]))
        publish(0, first, mid, i + 1, jnp.maximum(z, 0.0).astype(BF16))
        return c

    held, _ = sweep(make_first, lambda: send_rows(0, first, mid), FIRST)
    for dy in range(3):
        for dx in range(3):
            ws_ref[dy, :, dx * mid:(dx + 1) * mid] = spatial_ref[dy, dx]
            wc_ref[dy, dx, :heads, :] = class_ref[dy, dx]
            wc_ref[dy, dx, heads:, :] = jnp.zeros((outs - heads, chans), BF16)
    for h in range(rows):
        code = jnp.where(mask_ref[:, h, :] > 0, label_ref[:, h, :], 64)
        code_ref[h, :A, :] = code.astype(F32).astype(BF16)
        code_ref[h, A:, :] = jnp.ones((16 - A, cols), BF16)
    held = send_strip(0, first, mid, held)

    def turned(parts):
        size = parts[0].shape[1]
        eye = jnp.where(
            lax.broadcasted_iota(jnp.int32, (size, size), 0)
            == lax.broadcasted_iota(jnp.int32, (size, size), 1), 1.0, 0.0,
        ).astype(BF16)
        return dot_t(eye, jnp.concatenate(parts, axis=0)).astype(BF16)

    we_ref[...] = turned([wet_ref[...]])
    for dy in range(3):
        wsb_ref[dy] = turned([spatial_ref[2 - dy, 2 - dx] for dx in range(3)])
        wcb_ref[dy] = turned([wc_ref[2 - dy, 2 - dx] for dx in range(3)])
    widen(0, first, mid, held)

    def make_block(i, c):
        s = jnp.maximum(conv(lambda dy: ws_ref[dy], first, i, BLOCK[0]), 0.0).astype(BF16)
        spread_rows(second, i, s)
        b = jnp.maximum(cat(x_ref, i, BLOCK[0]).astype(F32) + dot(we_ref[...], s), 0.0)
        publish(1, block, chans, i + 1, b.astype(BF16))
        return c

    held, _ = sweep(make_block, lambda: send_rows(1, block, chans), BLOCK)
    held = send_strip(1, block, chans, held)
    widen(1, block, chans, held)

    def class_rows(dy):
        return jnp.concatenate([wc_ref[dy, dx] for dx in range(3)], axis=1)

    def make_dlog(i, carry):
        total, count = carry
        z = conv(class_rows, block, i, DLOG[0])
        code = cat(code_ref, i, DLOG[0])
        gap = dot(spread_ref[...], code)
        target = gap == 0.0
        alpha = jnp.where(target, -0.25, jnp.where(gap > 32.0, 0.0, 0.75))
        u = z * jnp.where(target, -LOG2E, LOG2E)
        e = jnp.exp2(-jnp.abs(u))
        soft = jnp.maximum(u, 0.0) + jnp.log2(1.0 + e)
        prob = jnp.exp2(u - soft)
        scaled = alpha * (prob * prob)
        terms = jnp.abs(scaled * soft)
        total = total + sum(terms[8 * k:8 * k + 8] for k in range(outs // 8))
        d = (scaled * ((2.0 * LN2 - 2.0 * LN2 * prob) * soft + prob)).astype(BF16)
        publish(2, dlog, outs, i + 1, d)
        spread_rows(dzero, i + 1, d)
        codes = code.astype(F32)
        row = lax.broadcasted_iota(jnp.int32, codes.shape, 0)
        hit = jnp.where((codes > 0.5) & (codes < 32.0) & (row < A), 1.0, 0.0)
        count = count + jnp.sum(hit, axis=0, keepdims=True)
        return total, count

    zero = jnp.zeros((1, DLOG[0] * cols), F32)
    zeros = jnp.zeros((8, DLOG[0] * cols), F32)
    held, (total, count) = sweep(
        make_dlog, lambda: send_rows(2, dlog, outs), DLOG, (zeros, zero)
    )
    total = jnp.sum(total, axis=0, keepdims=True)
    fold = lambda v: sum(v[:, k * 128:(k + 1) * 128] for k in range(v.shape[1] // 128))
    stat[0:1, :] = fold(total) * LN2
    stat[1:2, :] = fold(count)
    stat[2:, :] = jnp.zeros((6, 128), F32)

    def keep(value):
        stat[...] = value

    stats = reduce_whole(stat[...], *stat_slots, keep)
    advance(stats)
    held = send_strip(2, dlog, outs, held)

    def weight_sum(acc, grad, field, low, high):
        depth = grad.shape[1]
        acc[...] = jnp.zeros_like(acc)

        def add(i, c):
            at = i * WIDE + 1
            tall = jnp.concatenate([cat(grad, at + 1 - dy, WIDE) for dy in range(3)], axis=0)
            acc[...] += dot_t(tall, cat(field, at, WIDE, low, high))
            return c

        loop(rows // WIDE, add)
        acc[:depth, :] += dot_t(grad[1], field[0, low:high])
        acc[2 * depth:, :] += dot_t(grad[rows], field[rows + 1, low:high])

    bigs = []
    for dx in range(3):
        low, high = dx * chans, (dx + 1) * chans
        weight_sum(acc_c, dzero, block, low, high)
        send = big_refs[dx][0]
        for h in range(chans // 128):
            send[h * 3 * outs:(h + 1) * 3 * outs, :] = acc_c[
                :, h * 128:(h + 1) * 128
            ].astype(BF16)
        bigs.append(reduce_split(big_refs[dx]))
        advance(bigs[dx])
    widen(2, dlog, outs, held)

    def make_dsec(i, c):
        g = conv(lambda dy: wcb_ref[dy], dlog, i, DSEC[0])
        b = cat(block, i + 1, DSEC[0], chans, 2 * chans).astype(F32)
        ds = jnp.where(b > 0.0, g, 0.0).astype(BF16)
        s = cat(second, i, DSEC[0])
        acc_e[...] += dot_t(s, ds)
        h = dot(wet_ref[...], ds)
        d = jnp.where(s.astype(F32) > 0.0, h, 0.0).astype(BF16)
        publish(3, dsec, mid, i + 1, d)
        spread_rows(dsec_zero, i + 1, d)
        return c

    def after_edges():
        sent = send_rows(3, dsec, mid)
        advance(bigs[0], stats)
        return sent

    held, _ = sweep(make_dsec, after_edges, DSEC, halfway=lambda: advance(*bigs[1:]))
    held = send_strip(3, dsec, mid, held)
    advance(bigs[0], stats)
    weight_sum(acc_s, dsec_zero, first, 0, 3 * mid)
    mid_send, mid_full = mid_refs[:2]
    mid_send[:mid, :] = acc_e[...].astype(BF16)
    mid_send[mid:4 * mid, :3 * mid] = acc_s[...].astype(BF16)
    middle = reduce_split(mid_refs)
    advance(middle)
    advance(bigs[1])
    widen(3, dsec, mid, held)
    advance(bigs[2])

    def make_dfirst(i, c):
        g = conv(lambda dy: wsb_ref[dy], dsec, i, DFIRST)
        f = cat(first, i + 1, DFIRST, mid, 2 * mid).astype(F32)
        df = jnp.where(f > 0.0, g, 0.0).astype(BF16)
        acc_r[...] += dot_t(df, cat(x_ref, i, DFIRST))
        return c

    loop(rows // DFIRST, lambda j, c: make_dfirst(j * DFIRST, c))

    def place_tail(value):
        small_out[:mid, :] = value

    tail = reduce_whole(acc_r[...], *tail_refs, place_tail)
    advance(tail)
    scale = 1.0 / jnp.sum(stat[1:2, :], axis=1, keepdims=True)
    loss = jnp.sum(stat[0:1, :], axis=1, keepdims=True) * scale
    advance(middle)
    advance(tail)
    advance(middle)
    for dx in range(3):
        advance(bigs[dx])
        for h in range(chans // 128):
            for dy in range(3):
                at = (3 * h + dy) * outs
                class_out[dy, dx, :, h * 128:(h + 1) * 128] = (
                    big_refs[dx][1][at:at + outs, :].astype(F32) * scale
                )
    advance(middle)
    small_out[mid:2 * mid, :] = mid_full[:mid, :].astype(F32) * scale
    small_out[2 * mid:, :] = jnp.broadcast_to(loss, (8, chans))
    for dy in range(3):
        part = mid_full[(dy + 1) * mid:(dy + 2) * mid, :].astype(F32) * scale
        for dx in range(3):
            spatial_out[dy, dx] = part[:, dx * mid:(dx + 1) * mid]
    spatial_out[3] = jnp.zeros(spatial_out.shape[1:], F32)
    advance(tail)
    small_out[:mid, :] = small_out[:mid, :] * scale


def per_device(
    inputs, reduce_weight, spatial_weight, expand_weight, class_weight, anchor_labels, anchor_mask
):
    tiles, chans, rows, cols = inputs.shape
    assert tiles == 1
    mid = reduce_weight.shape[0]
    heads = class_weight.shape[2]
    outs = -(-heads // 16) * 16
    sizes = {axis: lax.axis_size(axis) for axis in AXES}

    x = inputs[0].transpose(1, 0, 2)

    spread = np.zeros((outs, 16), np.float32)
    spread[np.arange(heads), np.arange(heads) // K] = 1.0
    spread[np.arange(heads), A] = -1.0 - np.arange(heads) % K
    spread[heads:, A] = 64.0
    spread = jnp.asarray(spread, BF16)

    depths = (mid, chans, outs, mid)
    across = sizes["dp"] * sizes["col"]

    def split_refs(need, wide):
        piece = -(-need // (16 * across)) * 16
        full = pltpu.VMEM((piece * across, wide), BF16)
        return [full, full] + [
            pltpu.VMEM((count, piece, wide), BF16) for count in (across, sizes["row"])
        ]

    def whole_refs(shape, kind):
        return [pltpu.VMEM((count,) + shape, kind) for count in (across, sizes["row"])]

    copies = 16 + 6 * (across - 1) + 4 * (across - 1) + 6 * (sizes["row"] - 1)
    outputs = [
        ((2 * mid + 8, chans), F32), ((4, 3, mid, mid), F32), ((3, 3, outs, chans), F32)
    ]

    small, spatial, wide = pl.pallas_call(
        functools.partial(step_kernel, sizes, heads),
        out_shape=[jax.ShapeDtypeStruct(*output) for output in outputs],
        in_specs=[pl.BlockSpec(memory_space=pltpu.VMEM)] * 8,
        out_specs=[pl.BlockSpec(memory_space=pltpu.VMEM)] * 3,
        scratch_shapes=[
            pltpu.VMEM((rows + 2, 3 * mid, cols), BF16),
            pltpu.VMEM((rows, mid, cols), BF16),
            pltpu.VMEM((rows + 2, 3 * chans, cols), BF16),
            pltpu.VMEM((rows + 2, 3 * outs, cols), BF16),
            pltpu.VMEM((rows + 2, outs, cols), BF16),
            pltpu.VMEM((rows + 2, 3 * mid, cols), BF16),
            pltpu.VMEM((rows + 2, mid, cols), BF16),
            pltpu.VMEM((3 * outs, chans), F32),
            pltpu.VMEM((3 * mid, 3 * mid), F32),
            pltpu.VMEM((mid, chans), F32),
            pltpu.VMEM((mid, chans), F32),
            pltpu.VMEM((rows, 16, cols), BF16),
            pltpu.VMEM((3, mid, 3 * mid), BF16),
            pltpu.VMEM((3, mid, 3 * mid), BF16),
            pltpu.VMEM((chans, mid), BF16),
            pltpu.VMEM((3, 3, outs, chans), BF16),
            pltpu.VMEM((3, chans, 3 * outs), BF16),
            [pltpu.VMEM((depth, cols), BF16) for depth in depths],
            [pltpu.VMEM((2, depth, cols), BF16) for depth in depths],
            pltpu.VMEM((8, 128), F32),
            whole_refs((8, 128), F32),
            [split_refs(3 * outs * chans // 128, 128) for _ in range(3)],
            split_refs(4 * mid, chans),
            whole_refs((mid, chans), BF16),
            pltpu.SemaphoreType.DMA((copies,)),
            pltpu.SemaphoreType.DMA((copies,)),
        ],
        compiler_params=pltpu.CompilerParams(
            collective_id=1, has_side_effects=True, vmem_limit_bytes=36 * 1024 * 1024
        ),
        name="tile_step",
    )(
        x, anchor_labels[0], anchor_mask[0], spread, reduce_weight, spatial_weight,
        expand_weight.T, class_weight,
    )
    return (
        small[2 * mid, 0], small[:mid], spatial[:3], small[mid:2 * mid].T, wide[:, :, :heads]
    )


def solution(mesh):
    tiled = P("dp", None, "row", "col")
    return jax.shard_map(
        per_device,
        mesh=mesh,
        in_specs=(tiled, P(), P(), P(), P(), tiled, tiled),
        out_specs=(P(), P(), P(), P(), P()),
        check_vma=False,
    )
```
